128 devices in a mesh: gx: 8 (over z, x_hi), gy: 16 (over x_lo, y, core).
Axes of the slice: x: 4 (x_hi: 2, x_lo: 2; x = x_hi * 2 + x_lo), y: 4, z: 4, core: 2. Of those that a mesh axis runs over, the one named last changes fastest.
Arguments:
- source_planes: float32 [384, 384, 384], P(('gx', 'gy')), may hold values from -6 to 6
- weight_x: float32 [64, 384], replicated, may hold values from -0.3125 to 0.3125
- weight_y: float32 [96, 384], replicated, may hold values from -0.3125 to 0.3125
- weight_z: float32 [96, 384], replicated, may hold values from -0.3125 to 0.3125
- box_anchor: int32 [3], replicated, may hold values from 0 to 416, as said below
- velocity: float32 [3, 192, 512, 320], P(None, 'gx', 'gy'), may hold values from -6 to 6
- stress: float32 [6, 192, 512, 320], P(None, 'gx', 'gy'), may hold values from -6 to 6
- lame_lambda: float32 [192, 512, 320], P('gx', 'gy'), may hold values from 0.2 to 1
- lame_mu: float32 [192, 512, 320], P('gx', 'gy'), may hold values from 0.2 to 1
- buoyancy: float32 [192, 512, 320], P('gx', 'gy'), may hold values from 0.5 to 1.5
- attenuation: float32 [192, 512, 320], P('gx', 'gy'), may hold values from 0.05 to 3
Outputs:
- velocity_out: float32 [3, 192, 512, 320], P(None, 'gx', 'gy')
- stress_out: float32 [6, 192, 512, 320], P(None, 'gx', 'gy')
The draws below stay inside these ranges and needn't reach their ends.
Inputs may be any that keep to these rules, and one draw needn't show every extreme that they name: The box of 64 x 96 x 96 cells that starts at box_anchor lies inside the thorax grid; along the dimension with the most room it ends at the grid's far side, along one of the other two it starts at cell 0.
All inputs are finite; a program needn't handle non-finite values.
Results may differ from the reference program's by a relative error of at most 0.00005.
Values sent between devices are 32-bit elements; how exact they have to be, the bound alone decides.
No kernel may reach another device: no remote copies, remote signals or barrier semaphores. Data moves between devices by JAX's collectives and lax.ppermute only.
A program may use at most 128 MiB of HBM per device.

```python
import math
import jax
import jax.numpy as jnp
from jax import lax

SB = 384
BX = 64
BY = 96
BZ = 96
STEPS = 2
NX = 192
NY = 512
NZ = 320


def draw_box_anchor(key, part):
    keys = jax.random.split(key, 4)
    rooms = [NX - BX, NY - BY, NZ - BZ]
    largest = max(rooms)
    widest = 2 - rooms[::-1].index(largest)
    others = [which for which in range(3) if which != widest]
    first_zero = jax.random.randint(keys[3], (), 0, 2).astype(jnp.int32)
    draw_first = jax.random.randint(keys[others[0]], (), 0, rooms[others[0]] + 1).astype(jnp.int32)
    draw_second = jax.random.randint(keys[others[1]], (), 0, rooms[others[1]] + 1).astype(jnp.int32)
    zero_value = jnp.asarray(0, jnp.int32)
    value_first = jnp.where(first_zero == 1, zero_value, draw_first)
    value_second = jnp.where(first_zero == 1, draw_second, zero_value)
    entries = [None, None, None]
    entries[widest] = jnp.asarray(rooms[widest], jnp.int32)
    entries[others[0]] = value_first
    entries[others[1]] = value_second
    return jnp.stack(entries).astype(jnp.int32)


def level_of(rng, extent, cuts, smallest, high):
    factor_of = 1.0
    for dim, shards_of in cuts:
        heights = jax.random.uniform(jax.random.fold_in(jax.random.fold_in(rng, 6), dim), (shards_of,), jnp.float32, smallest / len(cuts), high / len(cuts))
        factor_of = factor_of * jnp.repeat(jnp.exp(heights), extent[dim] // shards_of).reshape((-1,) + (1,) * (len(extent) - 1 - dim))
    return factor_of


def normal_values(key, extent, width, limit, cuts=(), held_as=jnp.bfloat16):
    result = jax.random.normal(key, extent, jnp.float32) * width
    if len(cuts) > 0:
        result = level_of(key, extent, cuts, -0.22, 0.18) * result
    return jnp.clip(result, min=-limit, max=limit).astype(held_as)


def setup_inputs(seed: int = 0) -> dict:
    key_list = jax.random.split(jax.random.key(seed), 12)
    source_planes = normal_values(key_list[0], (SB, SB, SB), 1.0, 6.0, ((0, 128),), jnp.float32)
    weight_x = normal_values(key_list[1], (BX, SB), SB ** -0.5, 0.3125, (), jnp.float32)
    weight_y = normal_values(key_list[2], (BY, SB), SB ** -0.5, 0.3125, (), jnp.float32)
    weight_z = normal_values(key_list[3], (BZ, SB), SB ** -0.5, 0.3125, (), jnp.float32)
    box_anchor = draw_box_anchor(jax.random.fold_in(key_list[11], 71), 0)
    velocity = normal_values(key_list[5], (3, NX, NY, NZ), 1.0, 6.0, ((1, 8), (2, 16)), jnp.float32)
    stress = normal_values(key_list[6], (6, NX, NY, NZ), 1.0, 6.0, ((1, 8), (2, 16)), jnp.float32)
    lame_lambda = jnp.clip(jnp.exp(math.log(1.0) - 1.609438 * jax.random.uniform(key_list[7], (NX, NY, NZ), jnp.float32) ** level_of(key_list[7], (NX, NY, NZ), ((0, 8), (1, 16)), -0.2, 0.2)), 0.2, 1.0)
    lame_mu = jnp.clip(jnp.exp(math.log(1.0) - 1.609438 * jax.random.uniform(key_list[8], (NX, NY, NZ), jnp.float32) ** level_of(key_list[8], (NX, NY, NZ), ((0, 8), (1, 16)), -0.2, 0.2)), 0.2, 1.0)
    buoyancy = jnp.clip(jnp.exp(math.log(1.5) - 1.0986123 * jax.random.uniform(key_list[9], (NX, NY, NZ), jnp.float32) ** level_of(key_list[9], (NX, NY, NZ), ((0, 8), (1, 16)), -0.2, 0.2)), 0.5, 1.5)
    attenuation = jnp.clip(jnp.exp(math.log(3.0) - 4.0943445 * jax.random.uniform(key_list[10], (NX, NY, NZ), jnp.float32) ** level_of(key_list[10], (NX, NY, NZ), ((0, 8), (1, 16)), -0.2, 0.2)), 0.05, 3.0)
    return {"source_planes": source_planes, "weight_x": weight_x, "weight_y": weight_y, "weight_z": weight_z, "box_anchor": box_anchor, "velocity": velocity, "stress": stress, "lame_lambda": lame_lambda, "lame_mu": lame_mu, "buoyancy": buoyancy, "attenuation": attenuation}


time_step = 0.2
precise = lax.Precision.HIGHEST


def back_diff(values, dimension):
    count = values.shape[dimension]
    zeros = jnp.zeros_like(lax.slice_in_dim(values, 0, 1, axis=dimension))
    return values - jnp.concatenate([zeros, lax.slice_in_dim(values, 0, count - 1, axis=dimension)], dimension)


def ahead_diff(values, dimension):
    count = values.shape[dimension]
    zeros = jnp.zeros_like(lax.slice_in_dim(values, 0, 1, axis=dimension))
    return jnp.concatenate([lax.slice_in_dim(values, 1, count, axis=dimension), zeros], dimension) - values


def reference(source_planes, weight_x, weight_y, weight_z, box_anchor, velocity, stress, lame_lambda, lame_mu, buoyancy, attenuation):
    reduced = jnp.einsum('abc,zc->abz', source_planes, weight_z, precision=precise)
    reduced = jnp.einsum('abz,yb->ayz', reduced, weight_y, precision=precise)
    box = jnp.einsum('ayz,xa->xyz', reduced, weight_x, precision=precise)
    pressure = jnp.zeros(lame_mu.shape, jnp.float32)
    pressure = lax.dynamic_update_slice(pressure, box, (box_anchor[0].astype(jnp.int32), box_anchor[1].astype(jnp.int32), box_anchor[2].astype(jnp.int32)))
    decay = jnp.exp(-time_step * attenuation)
    speed_x, speed_y, speed_z = velocity[0], velocity[1], velocity[2]
    stress_xx, stress_yy, stress_zz = stress[0], stress[1], stress[2]
    stress_xy, stress_xz, stress_yz = stress[3], stress[4], stress[5]
    for stepping in range(STEPS):
        speed_x = speed_x + time_step * buoyancy * (back_diff(stress_xx, 0) + back_diff(stress_xy, 1) + back_diff(stress_xz, 2))
        speed_y = speed_y + time_step * buoyancy * (back_diff(stress_xy, 0) + back_diff(stress_yy, 1) + back_diff(stress_yz, 2))
        speed_z = speed_z + time_step * buoyancy * (back_diff(stress_xz, 0) + back_diff(stress_yz, 1) + back_diff(stress_zz, 2))
        strain_xx = ahead_diff(speed_x, 0)
        strain_yy = ahead_diff(speed_y, 1)
        strain_zz = ahead_diff(speed_z, 2)
        trace = strain_xx + strain_yy + strain_zz
        stress_xx = decay * (stress_xx + time_step * (lame_lambda * trace + 2.0 * lame_mu * strain_xx) - time_step * pressure)
        stress_yy = decay * (stress_yy + time_step * (lame_lambda * trace + 2.0 * lame_mu * strain_yy) - time_step * pressure)
        stress_zz = decay * (stress_zz + time_step * (lame_lambda * trace + 2.0 * lame_mu * strain_zz) - time_step * pressure)
        stress_xy = decay * (stress_xy + time_step * lame_mu * (ahead_diff(speed_x, 1) + ahead_diff(speed_y, 0)))
        stress_xz = decay * (stress_xz + time_step * lame_mu * (ahead_diff(speed_x, 2) + ahead_diff(speed_z, 0)))
        stress_yz = decay * (stress_yz + time_step * lame_mu * (ahead_diff(speed_y, 2) + ahead_diff(speed_z, 1)))
    velocity_out = jnp.stack([speed_x, speed_y, speed_z])
    stress_out = jnp.stack([stress_xx, stress_yy, stress_zz, stress_xy, stress_xz, stress_yz])
    return velocity_out, stress_out
```

```python
import functools

import jax
import jax.numpy as jnp
from jax import lax
from jax.experimental import pallas as pl
from jax.experimental.pallas import tpu as pltpu
from jax.sharding import PartitionSpec as P

time_step = 0.2
precise = lax.Precision.HIGHEST
planes_per_block = 4


def neighbour(value, axis, by):
    size = lax.axis_size(axis)
    pairs = [(i, i + by) for i in range(size) if 0 <= i + by < size]
    return lax.ppermute(value, axis, pairs)


def shifted_up(values, dimension, first):
    where = lax.broadcasted_iota(jnp.int32, values.shape, dimension)
    return jnp.where(where == 0, first, pltpu.roll(values, 1, dimension))


def shifted_down(values, dimension, last):
    count = values.shape[dimension]
    where = lax.broadcasted_iota(jnp.int32, values.shape, dimension)
    return jnp.where(where == count - 1, last, pltpu.roll(values, count - 1, dimension))


def velocity_kernel(with_source, *refs):
    if with_source:
        (stress, velocity, buoyancy, plane, rows, source, source_plane, source_rows) = refs[:8]
        out, first_plane, first_rows, carry = refs[8:]
    else:
        (stress, velocity, buoyancy, plane, rows) = refs[:5]
        out, first_plane, first_rows, carry = refs[5:]
    block = pl.program_id(0)

    @pl.when(block == 0)
    def _():
        carry[...] = plane[0:3]
        if with_source:
            carry[0] = plane[0] + source_plane[...]

    count = out.shape[1]
    before = [carry[0], carry[1], carry[2]]
    for t in range(count):
        s_xx, s_yy, s_zz = stress[0, t], stress[1, t], stress[2, t]
        s_xy, s_xz, s_yz = stress[3, t], stress[4, t], stress[5, t]
        row_xy, row_yy, row_yz = rows[t, 0:1], rows[t, 1:2], rows[t, 2:3]
        if with_source:
            extra = source[t]
            s_xx, s_yy, s_zz = s_xx + extra, s_yy + extra, s_zz + extra
            row_yy = row_yy + source_rows[t]
        factor = time_step * buoyancy[t]
        v_x = velocity[0, t] + factor * (
            (s_xx - before[0])
            + (s_xy - shifted_up(s_xy, 0, row_xy))
            + (s_xz - shifted_up(s_xz, 1, 0.0))
        )
        v_y = velocity[1, t] + factor * (
            (s_xy - before[1])
            + (s_yy - shifted_up(s_yy, 0, row_yy))
            + (s_yz - shifted_up(s_yz, 1, 0.0))
        )
        v_z = velocity[2, t] + factor * (
            (s_xz - before[2])
            + (s_yz - shifted_up(s_yz, 0, row_yz))
            + (s_zz - shifted_up(s_zz, 1, 0.0))
        )
        for c, v in enumerate((v_x, v_y, v_z)):
            out[c, t] = v
            first_rows[t, c : c + 1] = v[0:1]
        if t == 0:

            @pl.when(block == 0)
            def _():
                for c, v in enumerate((v_x, v_y, v_z)):
                    first_plane[c] = v

        before = [s_xx, s_xy, s_xz]
    for c in range(3):
        carry[c] = before[c]


def stress_kernel(with_source, *refs):
    if with_source:
        (stress, velocity, lame_lambda, lame_mu, attenuation, plane, rows, source) = refs[:8]
        out, carry = refs[8:]
    else:
        (stress, velocity, lame_lambda, lame_mu, attenuation, plane, rows) = refs[:7]
        out, last_plane, last_rows, carry = refs[7:]
    block = pl.program_id(0)

    @pl.when(block == 0)
    def _():
        carry[...] = plane[...]

    count = out.shape[1]
    after = [carry[0], carry[1], carry[2]]
    for t in reversed(range(count)):
        v = [velocity[0, t], velocity[1, t], velocity[2, t]]
        in_x = [after[c] - v[c] for c in range(3)]
        in_y = [shifted_down(v[c], 0, rows[t, c : c + 1]) - v[c] for c in range(3)]
        in_z = [shifted_down(v[c], 1, 0.0) - v[c] for c in range(3)]
        decay = jnp.exp(-time_step * attenuation[t])
        shear = time_step * lame_mu[t]
        common = time_step * lame_lambda[t] * (in_x[0] + in_y[1] + in_z[2])
        normal = [in_x[0], in_y[1], in_z[2]]
        values = []
        for c in range(3):
            value = stress[c, t] + common + 2.0 * shear * normal[c]
            if with_source:
                value = decay * (value + source[t]) + source[t]
            else:
                value = decay * value
            values.append(value)
        values.append(decay * (stress[3, t] + shear * (in_y[0] + in_x[1])))
        values.append(decay * (stress[4, t] + shear * (in_z[0] + in_x[2])))
        values.append(decay * (stress[5, t] + shear * (in_z[1] + in_y[2])))
        for c in range(6):
            out[c, t] = values[c]
        if not with_source:
            for c, which in enumerate((3, 1, 5)):
                last_rows[t, c : c + 1] = values[which][values[which].shape[0] - 1 :]
            if t == count - 1:

                @pl.when(block == 0)
                def _():
                    for c, which in enumerate((0, 3, 4)):
                        last_plane[c] = values[which]

        after = v
    for c in range(3):
        carry[c] = after[c]


def update_velocity(stress, velocity, buoyancy, plane, rows, source=None):
    _, nx, ny, nz = velocity.shape
    per = planes_per_block
    along = lambda g: (0, g, 0, 0)
    in_specs = [
        pl.BlockSpec((6, per, ny, nz), along),
        pl.BlockSpec((3, per, ny, nz), along),
        pl.BlockSpec((per, ny, nz), lambda g: (g, 0, 0)),
        pl.BlockSpec(plane.shape, lambda g: (0, 0, 0)),
        pl.BlockSpec((per,) + rows.shape[1:], lambda g: (g, 0, 0)),
    ]
    args = [stress, velocity, buoyancy, plane, rows]
    if source is not None:
        in_specs += [
            pl.BlockSpec((per, ny, nz), lambda g: (g, 0, 0)),
            pl.BlockSpec((ny, nz), lambda g: (0, 0)),
            pl.BlockSpec((per, 1, nz), lambda g: (g, 0, 0)),
        ]
        args += list(source)
    cells = nx * ny * nz
    return pl.pallas_call(
        functools.partial(velocity_kernel, source is not None),
        grid=(nx // per,),
        in_specs=in_specs,
        out_specs=(
            pl.BlockSpec((3, per, ny, nz), along),
            pl.BlockSpec((3, ny, nz), lambda g: (0, 0, 0)),
            pl.BlockSpec((per, 3, nz), lambda g: (g, 0, 0)),
        ),
        out_shape=(
            jax.ShapeDtypeStruct(velocity.shape, jnp.float32),
            jax.ShapeDtypeStruct((3, ny, nz), jnp.float32),
            jax.ShapeDtypeStruct((nx, 3, nz), jnp.float32),
        ),
        scratch_shapes=[pltpu.VMEM((3, ny, nz), jnp.float32)],
        cost_estimate=pl.CostEstimate(
            flops=40 * cells, bytes_accessed=4 * 14 * cells, transcendentals=0
        ),
        name="velocity_second" if source is not None else "velocity_first",
    )(*args)


def update_stress(stress, velocity, coefficients, plane, rows, source=None):
    _, nx, ny, nz = velocity.shape
    per = planes_per_block
    blocks = nx // per
    along = lambda g: (0, blocks - 1 - g, 0, 0)
    cell = lambda g: (blocks - 1 - g, 0, 0)
    in_specs = [
        pl.BlockSpec((6, per, ny, nz), along),
        pl.BlockSpec((3, per, ny, nz), along),
        pl.BlockSpec((per, ny, nz), cell),
        pl.BlockSpec((per, ny, nz), cell),
        pl.BlockSpec((per, ny, nz), cell),
        pl.BlockSpec((3, ny, nz), lambda g: (0, 0, 0)),
        pl.BlockSpec((per, 3, nz), cell),
    ]
    args = [stress, velocity, *coefficients, plane, rows]
    out_specs = [pl.BlockSpec((6, per, ny, nz), along)]
    out_shape = [jax.ShapeDtypeStruct(stress.shape, jnp.float32)]
    if source is not None:
        in_specs.append(pl.BlockSpec((per, ny, nz), cell))
        args.append(source)
    else:
        out_specs += [
            pl.BlockSpec((3, ny, nz), lambda g: (0, 0, 0)),
            pl.BlockSpec((per, 3, nz), cell),
        ]
        out_shape += [
            jax.ShapeDtypeStruct((3, ny, nz), jnp.float32),
            jax.ShapeDtypeStruct((nx, 3, nz), jnp.float32),
        ]
    cells = nx * ny * nz
    return pl.pallas_call(
        functools.partial(stress_kernel, source is not None),
        grid=(blocks,),
        in_specs=in_specs,
        out_specs=tuple(out_specs),
        out_shape=tuple(out_shape),
        scratch_shapes=[pltpu.VMEM((3, ny, nz), jnp.float32)],
        cost_estimate=pl.CostEstimate(
            flops=60 * cells, bytes_accessed=4 * 18 * cells, transcendentals=cells
        ),
        name="stress_second" if source is not None else "stress_first",
    )(*args)


def shards(
    source_planes,
    weight_x,
    weight_y,
    weight_z,
    box_anchor,
    velocity,
    stress,
    lame_lambda,
    lame_mu,
    buoyancy,
    attenuation,
):
    nx, ny, nz = lame_mu.shape
    box_x, sources = weight_x.shape
    box_y, box_z = weight_y.shape[0], weight_z.shape[0]
    size_x, size_y = lax.axis_size("gx"), lax.axis_size("gy")
    columns = box_y // ny
    part = ny // size_x

    send_x = jnp.stack([stress[0, -1], stress[3, -1], stress[4, -1], attenuation[-1]])
    send_y = jnp.stack(
        [stress[3, :, -1], stress[1, :, -1], stress[5, :, -1], attenuation[:, -1]], axis=1
    )
    plane = neighbour(send_x, "gx", 1)
    rows = neighbour(send_y, "gy", 1)

    reduced = jnp.einsum("abc,zc->abz", source_planes, weight_z, precision=precise)
    reduced = jnp.einsum("abz,yb->ayz", reduced, weight_y, precision=precise)
    own = reduced.shape[0]
    padded = jnp.pad(reduced, ((0, 0), (1, 0), (0, 0)))
    pieces = []
    for i in range(size_x):
        for k in range(columns):
            start = k * ny + i * part
            pieces.append(padded[:, start : start + part + 1])
    pieces = jnp.stack(pieces).reshape(size_x, columns, own * (part + 1), box_z)
    pieces = jnp.pad(pieces, ((0, 0), (size_y - columns, 0), (0, 0), (0, 0)))
    pieces = pieces.reshape(size_x * size_y, own * (part + 1), box_z)

    speed, edge_x, edge_y = update_velocity(stress, velocity, buoyancy, plane, rows)
    upper_x = neighbour(edge_x, "gx", -1)
    upper_y = neighbour(edge_y, "gy", -1)

    gathered = lax.all_to_all(pieces, ("gx", "gy"), 0, 0, tiled=True)
    gathered = gathered.reshape(sources, part + 1, box_z)
    placed = jnp.zeros((size_x * nx + 1, sources), jnp.float32)
    placed = lax.dynamic_update_slice(placed, weight_x, (box_anchor[0] + 1, 0))
    windows = jnp.stack([placed[i * nx : i * nx + nx + 1] for i in range(size_x)])
    shares = jnp.einsum("ixa,arz->ixrz", windows, gathered, precision=precise)

    coefficients = (lame_lambda, lame_mu, attenuation)
    strained, edge_x, edge_y = update_stress(stress, speed, coefficients, upper_x, upper_y)
    lower_x = neighbour(edge_x, "gx", 1)
    lower_y = neighbour(edge_y, "gy", 1)

    box = lax.all_to_all(shares, "gx", 0, 0, tiled=True)

    def place(values):
        out = jnp.zeros(values.shape[:-1] + (nz,), jnp.float32)
        start = (0,) * (values.ndim - 1) + (box_anchor[2],)
        return lax.dynamic_update_slice(out, values, start)

    def lost(values, rate):
        return -time_step * jnp.exp(-time_step * rate) * values

    inner = box[:, 1:, 1:].transpose(1, 0, 2, 3).reshape(nx, ny, box_z)
    source = lost(place(inner), attenuation)
    source_plane = lost(place(box[:, 0, 1:].reshape(ny, box_z)), plane[3])
    source_rows = lost(place(box[0, 1:, 0]), rows[:, 3])[:, None]

    speed, edge_x, edge_y = update_velocity(
        strained, speed, buoyancy, lower_x, lower_y, (source, source_plane, source_rows)
    )
    upper_x = neighbour(edge_x, "gx", -1)
    upper_y = neighbour(edge_y, "gy", -1)
    (strained,) = update_stress(strained, speed, coefficients, upper_x, upper_y, source)
    return (speed, strained)


def solution(mesh):
    in_specs = (
        P(("gx", "gy"), None, None),
        P(),
        P(),
        P(),
        P(),
        P(None, "gx", "gy", None),
        P(None, "gx", "gy", None),
        P("gx", "gy", None),
        P("gx", "gy", None),
        P("gx", "gy", None),
        P("gx", "gy", None),
    )
    out_specs = (P(None, "gx", "gy", None), P(None, "gx", "gy", None))
    return jax.shard_map(shards, mesh=mesh, in_specs=in_specs, out_specs=out_specs, check_vma=False)
```

```python
import functools

import jax
import jax.numpy as jnp
from jax import lax
from jax.experimental import pallas as pl
from jax.experimental.pallas import tpu as pltpu
from jax.sharding import PartitionSpec as P

time_step = 0.2
precise = lax.Precision.HIGHEST
strip = 8
lanes = 128
per = 6


def neighbour(value, axis, by):
    size = lax.axis_size(axis)
    pairs = [(i, i + by) for i in range(size) if 0 <= i + by < size]
    return lax.ppermute(value, axis, pairs)


def f32(*shape):
    return jax.ShapeDtypeStruct(shape, jnp.float32)


def dot(a, b, contract=((1,), (0,))):
    return lax.dot_general(
        a, b, (contract, ((), ())), precision=precise, preferred_element_type=jnp.float32
    )


def shifted_up(values):
    first = jnp.zeros((values.shape[0], 1), jnp.float32)
    return jnp.concatenate([first, values[:, :-1]], 1)


def shifted_down(values):
    last = jnp.zeros((values.shape[0], 1), jnp.float32)
    return jnp.concatenate([values[:, 1:], last], 1)


def after_row(values, row):
    where = lax.broadcasted_iota(jnp.int32, values.shape, 0)
    return jnp.where(where == 0, row, pltpu.roll(values, 1, 0))


def edges_kernel(plane, rate_plane, tile, rate_tile, out_plane, out_rows):
    for c, which in enumerate((0, 3, 4)):
        out_plane[c] = plane[which, 0]
    out_plane[3] = rate_plane[0]
    for c, which in enumerate((3, 1, 5)):
        out_rows[c] = tile[which, :, strip - 1]
    out_rows[3] = rate_tile[:, strip - 1]


def edges(stress, attenuation):
    _, nx, ny, nz = stress.shape
    last = ny // strip - 1
    return pl.pallas_call(
        edges_kernel,
        grid=(1,),
        in_specs=[
            pl.BlockSpec((6, 1, ny, nz), lambda g: (0, nx - 1, 0, 0)),
            pl.BlockSpec((1, ny, nz), lambda g: (nx - 1, 0, 0)),
            pl.BlockSpec((6, nx, strip, nz), lambda g: (0, 0, last, 0)),
            pl.BlockSpec((nx, strip, nz), lambda g: (0, last, 0)),
        ],
        out_specs=(
            pl.BlockSpec((4, ny, nz), lambda g: (0, 0, 0)),
            pl.BlockSpec((4, nx, nz), lambda g: (0, 0, 0)),
        ),
        out_shape=(f32(4, ny, nz), f32(4, nx, nz)),
        compiler_params=pltpu.CompilerParams(vmem_limit_bytes=12 << 20),
        name="edges",
    )(stress, attenuation, stress, attenuation)


def sections_kernel(size_x, size_y, columns, planes, weight_y, weight_z, out, held):
    own = planes.shape[0]
    box_y, box_z = weight_y.shape[0], weight_z.shape[0]
    part = box_y // (columns * size_x)
    out[...] = jnp.zeros_like(out)
    held[...] = jnp.zeros_like(held)
    for t in range(own):
        partly = dot(weight_y[...], planes[t])
        held[t, strip : strip + box_y, :box_z] = dot(partly, weight_z[...], ((1,), (1,)))
    for k in range(columns):
        for i in range(size_x):
            start = strip + (k * size_x + i) * part - 1
            for t in range(own):
                piece = held[t, start : start + part + 1]
                row = t * (part + 1)
                out[i * size_y + size_y - columns + k, row : row + part + 1] = piece


def sections(planes, weight_y, weight_z, size_x, size_y, columns, height):
    own = planes.shape[0]
    return pl.pallas_call(
        functools.partial(sections_kernel, size_x, size_y, columns),
        out_shape=f32(size_x * size_y, height, lanes),
        scratch_shapes=[pltpu.VMEM((own, strip + weight_y.shape[0], lanes), jnp.float32)],
        compiler_params=pltpu.CompilerParams(vmem_limit_bytes=16 << 20),
        name="sections",
    )(planes, weight_y, weight_z)


def contract_kernel(own, part, nx, anchor, weight_x, gathered, out, padded):
    box_x, count = weight_x.shape
    size_x, height, _ = out.shape
    rows = height // (part + 1)
    devices = count // own
    stride = gathered.shape[0] // devices
    section = lax.broadcasted_iota(jnp.int32, (count, count), 0)
    column = lax.broadcasted_iota(jnp.int32, (count, count), 1)
    pick = section == own * lax.rem(column, devices) + lax.div(column, devices)
    weights = dot(weight_x[...], pick.astype(jnp.float32))
    padded[...] = jnp.zeros_like(padded)
    for r in range(part + 1):
        terms = [
            gathered[pl.ds(t * (part + 1) + r, devices, stride=stride), :] for t in range(own)
        ]
        box = dot(weights, jnp.concatenate(terms, 0))
        padded[r, pl.ds(anchor[0] + strip, box_x), :] = box
    for i in range(size_x):
        start = strip + i * nx
        for r in range(part + 1):
            out[i, r * rows : r * rows + nx] = padded[r, start : start + nx]
            out[i, r * rows + nx : (r + 1) * rows] = padded[r, start - 1 : start - 1 + rows - nx]


def contract(anchor, weight_x, gathered, own, part, nx, size_x, rows):
    return pl.pallas_call(
        functools.partial(contract_kernel, own, part, nx),
        in_specs=[
            pl.BlockSpec(memory_space=pltpu.SMEM),
            pl.BlockSpec(memory_space=pltpu.VMEM),
            pl.BlockSpec(memory_space=pltpu.VMEM),
        ],
        out_shape=f32(size_x, (part + 1) * rows, lanes),
        scratch_shapes=[pltpu.VMEM((part + 1, 2 * strip + size_x * nx, lanes), jnp.float32)],
        compiler_params=pltpu.CompilerParams(vmem_limit_bytes=16 << 20),
        name="contract",
    )(anchor, weight_x, gathered)


def place_kernel(part, anchor, box, rate, rate_plane, rate_rows, out, out_plane, out_rows, held):
    size_x, height, _ = box.shape
    nx, ny, nz = out.shape
    rows = height // (part + 1)
    for i in range(size_x):
        for r in range(part):
            y = i * part + r
            first = (r + 1) * rows
            held[pl.ds(y, nx, stride=ny), :] = box[i, first : first + nx]
            held[nx * ny + y : nx * ny + y + 1] = box[i, first + nx : first + nx + 1]
    cell = lax.broadcasted_iota(jnp.int32, (lanes, nz), 1)
    which = lax.broadcasted_iota(jnp.int32, (lanes, nz), 0)
    pick = (cell - anchor[2] == which).astype(jnp.float32)

    def lost(values, rates):
        return (-time_step) * jnp.exp(-time_step * rates) * dot(values, pick)

    for t in range(0, nx, 4):
        values = (-time_step) * dot(held[t * ny : (t + 4) * ny], pick)
        for s in range(4):
            decay = jnp.exp(-time_step * rate[t + s])
            out[t + s] = decay * values[s * ny : (s + 1) * ny]
    out_plane[...] = lost(held[nx * ny :], rate_plane[3])
    out_rows[...] = lost(box[0, 0:nx], rate_rows[3])


def place(anchor, box, rate, rate_plane, rate_rows, part):
    nx, ny, nz = rate.shape
    return pl.pallas_call(
        functools.partial(place_kernel, part),
        in_specs=[pl.BlockSpec(memory_space=pltpu.SMEM)]
        + [pl.BlockSpec(memory_space=pltpu.VMEM)] * 4,
        out_shape=(f32(nx, ny, nz), f32(ny, nz), f32(nx, nz)),
        scratch_shapes=[pltpu.VMEM(((nx + 1) * ny, lanes), jnp.float32)],
        compiler_params=pltpu.CompilerParams(vmem_limit_bytes=16 << 20),
        name="place",
    )(anchor, box, rate, rate_plane, rate_rows)


def first_kernel(with_source, *refs):
    if with_source:
        (s_plane, v_plane, b_plane, s_tile, v_tile, b_tile, plane, rows) = refs[:8]
        q_plane, q_tile, source_plane, source_rows = refs[8:12]
    else:
        (s_plane, v_plane, b_plane, s_tile, v_tile, b_tile, plane, rows) = refs[:8]
    out_plane, out_rows = refs[-2:]
    low = [plane[c] for c in range(3)]
    edge = [rows[c] for c in range(3)]
    in_plane = [s_plane[c, 0] for c in range(6)]
    in_rows = [s_tile[c, :, 0] for c in range(6)]
    if with_source:
        low[0] = low[0] + source_plane[...]
        edge[1] = edge[1] + source_rows[...]
        for c in range(3):
            in_plane[c] = in_plane[c] + q_plane[0]
            in_rows[c] = in_rows[c] + q_tile[:, 0]

    xx, yy, zz, xy, xz, yz = in_plane
    factor = time_step * b_plane[0]
    head = [value[0:1] for value in edge]
    out_plane[0] = v_plane[0, 0] + factor * (
        (xx - low[0]) + (xy - after_row(xy, head[0])) + (xz - shifted_up(xz))
    )
    out_plane[1] = v_plane[1, 0] + factor * (
        (xy - low[1]) + (yy - after_row(yy, head[1])) + (yz - shifted_up(yz))
    )
    out_plane[2] = v_plane[2, 0] + factor * (
        (xz - low[2]) + (yz - after_row(yz, head[2])) + (zz - shifted_up(zz))
    )
    xx, yy, zz, xy, xz, yz = in_rows
    factor = time_step * b_tile[:, 0]
    head = [value[0:1] for value in low]
    out_rows[0] = v_tile[0, :, 0] + factor * (
        (xx - after_row(xx, head[0])) + (xy - edge[0]) + (xz - shifted_up(xz))
    )
    out_rows[1] = v_tile[1, :, 0] + factor * (
        (xy - after_row(xy, head[1])) + (yy - edge[1]) + (yz - shifted_up(yz))
    )
    out_rows[2] = v_tile[2, :, 0] + factor * (
        (xz - after_row(xz, head[2])) + (yz - edge[2]) + (zz - shifted_up(zz))
    )


def first_edges(stress, velocity, buoyancy, plane, rows, source=None):
    _, nx, ny, nz = velocity.shape
    fixed = lambda *shape: pl.BlockSpec(shape, lambda g: (0,) * len(shape))
    in_specs = [
        fixed(6, 1, ny, nz),
        fixed(3, 1, ny, nz),
        fixed(1, ny, nz),
        fixed(6, nx, strip, nz),
        fixed(3, nx, strip, nz),
        fixed(nx, strip, nz),
        fixed(*plane.shape),
        fixed(*rows.shape),
    ]
    args = [stress, velocity, buoyancy, stress, velocity, buoyancy, plane, rows]
    if source is not None:
        in_specs += [fixed(1, ny, nz), fixed(nx, strip, nz), fixed(ny, nz), fixed(nx, nz)]
        args += [source[0], *source]
    return pl.pallas_call(
        functools.partial(first_kernel, source is not None),
        grid=(1,),
        in_specs=in_specs,
        out_specs=(fixed(3, ny, nz), fixed(3, nx, nz)),
        out_shape=(f32(3, ny, nz), f32(3, nx, nz)),
        compiler_params=pltpu.CompilerParams(vmem_limit_bytes=16 << 20),
        cost_estimate=pl.CostEstimate(
            flops=80 * nz * (nx + ny), bytes_accessed=4 << 20, transcendentals=0
        ),
        name="first_edges",
    )(*args)


def step_kernel(with_source, *refs):
    (stress, velocity, buoyancy, lame_lambda, lame_mu, attenuation) = refs[:6]
    (below_xx, below_xy, below_xz, plane, rows, upper_plane, upper_rows) = refs[6:13]
    if with_source:
        source, below_source, source_plane, source_rows = refs[13:17]
        new_velocity, new_stress, carry = refs[17:]
    else:
        new_velocity, new_stress, last_plane, last_rows, carry = refs[13:]
    _, count, ny, nz = new_velocity.shape
    step = pl.program_id(0)
    block = pl.num_programs(0) - 1 - step
    carry_v, carry_s = carry.at[0:3], carry.at[3:6]

    @pl.when(step == 0)
    def _():
        for c in range(3):
            carry_v[c] = upper_plane[c]

    @pl.when(block == 0)
    def _():
        for c in range(3):
            carry_s[c] = plane[c]
        if with_source:
            carry_s[0] = plane[0] + source_plane[...]

    @pl.when(block != 0)
    def _():
        carry_s[0] = below_xx[0, 0]
        if with_source:
            carry_s[0] = below_xx[0, 0] + below_source[0]
        carry_s[1] = below_xy[0, 0]
        carry_s[2] = below_xz[0, 0]

    top = lax.broadcasted_iota(jnp.int32, (strip, nz), 0) == 0
    bottom = lax.broadcasted_iota(jnp.int32, (strip, nz), 0) == strip - 1

    def velocity_plane(t, _):
        x = block * count + t
        above = [rows[c, pl.ds(x, 1)] for c in range(3)]
        if with_source:
            above[1] = above[1] + source_rows[pl.ds(x, 1)]
        above = [jnp.broadcast_to(row, (strip, nz)) for row in above]
        for r in range(ny // strip):
            here = slice(strip * r, strip * (r + 1))
            s = [stress[c, t, here] for c in range(6)]
            if with_source:
                extra = source[t, here]
                s[:3] = [value + extra for value in s[:3]]
            s_xx, s_yy, s_zz, s_xy, s_xz, s_yz = s
            before = [carry_s[c, here] for c in range(3)]
            rolled = [pltpu.roll(value, 1, 0) for value in (s_xy, s_yy, s_yz)]
            up = [jnp.where(top, above[c], rolled[c]) for c in range(3)]
            factor = time_step * buoyancy[t, here]
            sums = (
                (s_xx - before[0]) + (s_xy - up[0]) + (s_xz - shifted_up(s_xz)),
                (s_xy - before[1]) + (s_yy - up[1]) + (s_yz - shifted_up(s_yz)),
                (s_xz - before[2]) + (s_yz - up[2]) + (s_zz - shifted_up(s_zz)),
            )
            for c in range(3):
                new_velocity[c, t, here] = velocity[c, t, here] + factor * sums[c]
            for c, value in enumerate((s_xx, s_xy, s_xz)):
                carry_s[c, here] = value
            above = rolled
        return 0

    def stress_plane(back, _):
        t = count - 1 - back
        x = block * count + t
        below = [jnp.broadcast_to(upper_rows[c, pl.ds(x, 1)], (strip, nz)) for c in range(3)]
        for r in reversed(range(ny // strip)):
            here = slice(strip * r, strip * (r + 1))
            v = [new_velocity[c, t, here] for c in range(3)]
            rolled = [pltpu.roll(value, strip - 1, 0) for value in v]
            in_x = [carry_v[c, here] - v[c] for c in range(3)]
            in_y = [jnp.where(bottom, below[c], rolled[c]) - v[c] for c in range(3)]
            in_z = [shifted_down(v[c]) - v[c] for c in range(3)]
            decay = jnp.exp(-time_step * attenuation[t, here])
            shear = time_step * lame_mu[t, here]
            normal = [in_x[0], in_y[1], in_z[2]]
            common = time_step * lame_lambda[t, here] * (normal[0] + normal[1] + normal[2])
            twice = 2.0 * shear
            if with_source:
                extra = source[t, here]
                common = common + extra
            values = []
            for c in range(3):
                value = decay * (stress[c, t, here] + (common + twice * normal[c]))
                values.append(value + extra if with_source else value)
            values.append(decay * (stress[3, t, here] + shear * (in_y[0] + in_x[1])))
            values.append(decay * (stress[4, t, here] + shear * (in_z[0] + in_x[2])))
            values.append(decay * (stress[5, t, here] + shear * (in_z[1] + in_y[2])))
            for c in range(6):
                new_stress[c, t, here] = values[c]
            if not with_source and r == ny // strip - 1:
                for c, which in enumerate((3, 1, 5)):
                    last_rows[c, pl.ds(x, 1)] = values[which][strip - 1 :]
            for c in range(3):
                carry_v[c, here] = v[c]
            below = rolled
        return 0

    lax.fori_loop(0, count, velocity_plane, 0)
    lax.fori_loop(0, count, stress_plane, 0)
    if not with_source:

        @pl.when(step == 0)
        def _():
            for c, which in enumerate((0, 3, 4)):
                last_plane[c] = new_stress[which, count - 1]


def full_step(stress, velocity, coefficients, plane, rows, upper_plane, upper_rows, source=None):
    _, nx, ny, nz = velocity.shape
    blocks = nx // per
    field = lambda g: (0, blocks - 1 - g, 0, 0)
    cell = lambda g: (blocks - 1 - g, 0, 0)
    under = lambda g: jnp.maximum((blocks - 1 - g) * per - 1, 0)
    fixed = lambda *shape: pl.BlockSpec(shape, lambda g: (0,) * len(shape))
    in_specs = [
        pl.BlockSpec((6, per, ny, nz), field),
        pl.BlockSpec((3, per, ny, nz), field),
        *[pl.BlockSpec((per, ny, nz), cell)] * 4,
        *[pl.BlockSpec((1, 1, ny, nz), lambda g, c=c: (c, under(g), 0, 0)) for c in (0, 3, 4)],
        fixed(*plane.shape),
        fixed(*rows.shape),
        fixed(*upper_plane.shape),
        fixed(*upper_rows.shape),
    ]
    args = [stress, velocity, *coefficients, stress, stress, stress]
    args += [plane, rows, upper_plane, upper_rows]
    out_specs = [pl.BlockSpec((3, per, ny, nz), field), pl.BlockSpec((6, per, ny, nz), field)]
    out_shape = [f32(*velocity.shape), f32(*stress.shape)]
    if source is not None:
        in_specs += [
            pl.BlockSpec((per, ny, nz), cell),
            pl.BlockSpec((1, ny, nz), lambda g: (under(g), 0, 0)),
            fixed(ny, nz),
            fixed(nx, nz),
        ]
        args += [source[0], *source]
    else:
        out_specs += [fixed(3, ny, nz), fixed(3, nx, nz)]
        out_shape += [f32(3, ny, nz), f32(3, nx, nz)]
    cells = nx * ny * nz
    return pl.pallas_call(
        functools.partial(step_kernel, source is not None),
        grid=(blocks,),
        in_specs=in_specs,
        out_specs=tuple(out_specs),
        out_shape=tuple(out_shape),
        scratch_shapes=[pltpu.VMEM((6, ny, nz), jnp.float32)],
        compiler_params=pltpu.CompilerParams(vmem_limit_bytes=32 << 20),
        cost_estimate=pl.CostEstimate(
            flops=100 * cells, bytes_accessed=4 * 23 * cells, transcendentals=cells
        ),
        name="second_step" if source is not None else "first_step",
    )(*args)


def shards(
    source_planes,
    weight_x,
    weight_y,
    weight_z,
    box_anchor,
    velocity,
    stress,
    lame_lambda,
    lame_mu,
    buoyancy,
    attenuation,
):
    nx, ny, nz = lame_mu.shape
    box_x, sources = weight_x.shape
    box_y = weight_y.shape[0]
    size_x, size_y = lax.axis_size("gx"), lax.axis_size("gy")
    own = source_planes.shape[0]
    columns = box_y // ny
    part = ny // size_x
    height = -(-own * (part + 1) // strip) * strip
    coefficients = (buoyancy, lame_lambda, lame_mu, attenuation)

    send_x, send_y = edges(stress, attenuation)
    plane = neighbour(send_x, "gx", 1)
    rows = neighbour(send_y, "gy", 1)

    pieces = sections(source_planes, weight_y, weight_z, size_x, size_y, columns, height)
    gathered = lax.all_to_all(pieces, ("gx", "gy"), 0, 0, tiled=True)

    first_x, first_y = first_edges(stress, velocity, buoyancy, plane, rows)
    upper_x = neighbour(first_x, "gx", -1)
    upper_y = neighbour(first_y, "gy", -1)

    gathered = gathered.reshape(size_x * size_y * height, lanes)
    shares = contract(box_anchor, weight_x, gathered, own, part, nx, size_x, nx + strip)
    box = lax.all_to_all(shares, "gx", 0, 0, tiled=True)

    speed, strained, last_x, last_y = full_step(
        stress, velocity, coefficients, plane, rows, upper_x, upper_y
    )
    lower_x = neighbour(last_x, "gx", 1)
    lower_y = neighbour(last_y, "gy", 1)

    source = place(box_anchor, box, attenuation, plane, rows, part)
    first_x, first_y = first_edges(strained, speed, buoyancy, lower_x, lower_y, source)
    upper_x = neighbour(first_x, "gx", -1)
    upper_y = neighbour(first_y, "gy", -1)
    return tuple(
        full_step(
            strained, speed, coefficients, lower_x, lower_y, upper_x, upper_y, source
        )
    )


def solution(mesh):
    in_specs = (
        P(("gx", "gy"), None, None),
        P(),
        P(),
        P(),
        P(),
        P(None, "gx", "gy", None),
        P(None, "gx", "gy", None),
        P("gx", "gy", None),
        P("gx", "gy", None),
        P("gx", "gy", None),
        P("gx", "gy", None),
    )
    out_specs = (P(None, "gx", "gy", None), P(None, "gx", "gy", None))
    return jax.shard_map(shards, mesh=mesh, in_specs=in_specs, out_specs=out_specs, check_vma=False)
```

```python
import functools

import jax
import jax.numpy as jnp
from jax import lax
from jax.experimental import pallas as pl
from jax.experimental.pallas import tpu as pltpu
from jax.sharding import PartitionSpec as P

time_step = 0.2
precise = lax.Precision.HIGHEST
strip = 8
lanes = 128
per = 3


def neighbour(value, axis, by):
    size = lax.axis_size(axis)
    pairs = [(i, i + by) for i in range(size) if 0 <= i + by < size]
    return lax.ppermute(value, axis, pairs)


def in_hbm(value):
    return pltpu.with_memory_space_constraint(value, pltpu.HBM)


def in_vmem(value):
    return pltpu.with_memory_space_constraint(value, pltpu.VMEM)


def f32(*shape):
    return jax.ShapeDtypeStruct(shape, jnp.float32)


def dot(a, b, contract=((1,), (0,))):
    return lax.dot_general(
        a, b, (contract, ((), ())), precision=precise, preferred_element_type=jnp.float32
    )


def shifted_up(values):
    first = jnp.zeros((values.shape[0], 1), jnp.float32)
    return jnp.concatenate([first, values[:, :-1]], 1)


def shifted_down(values):
    last = jnp.zeros((values.shape[0], 1), jnp.float32)
    return jnp.concatenate([values[:, 1:], last], 1)


def after_row(values, row):
    where = lax.broadcasted_iota(jnp.int32, values.shape, 0)
    return jnp.where(where == 0, row, pltpu.roll(values, 1, 0))


def partial_velocity(stress, velocity, factor, out, before):
    xx, yy, zz, xy, xz, yz = stress
    along_x, along_y = before
    out[0] = velocity[0] + factor * (
        (xx - along_x(xx)) + (xy - along_y(xy)) + (xz - shifted_up(xz))
    )
    out[1] = velocity[1] + factor * (
        (xy - along_x(xy)) + (yy - along_y(yy)) + (yz - shifted_up(yz))
    )
    out[2] = velocity[2] + factor * (
        (xz - along_x(xz)) + (yz - along_y(yz)) + (zz - shifted_up(zz))
    )


def nothing(values):
    return jnp.zeros_like(values)


def row_before(values):
    return after_row(values, 0.0)


def edges_kernel(stress, velocity, buoyancy, attenuation, *refs):
    out_plane, out_rows, part_plane, part_rows, b_plane, b_rows = refs[:6]
    s_plane, s_rows, v_plane, v_rows, sems = refs[6:]
    _, nx, ny, _ = stress.shape
    moves = [
        (stress.at[:, 0], s_plane),
        (stress.at[:, :, 0], s_rows),
        (velocity.at[:, 0], v_plane),
        (velocity.at[:, :, 0], v_rows),
        (buoyancy.at[0], b_plane),
        (buoyancy.at[:, 0], b_rows),
        (stress.at[0, nx - 1], out_plane.at[0]),
        (stress.at[3:5, nx - 1], out_plane.at[1:3]),
        (attenuation.at[nx - 1], out_plane.at[3]),
        (stress.at[3, :, ny - 1], out_rows.at[0]),
        (stress.at[1, :, ny - 1], out_rows.at[1]),
        (stress.at[5, :, ny - 1], out_rows.at[2]),
        (attenuation.at[:, ny - 1], out_rows.at[3]),
    ]
    copies = [pltpu.make_async_copy(*move, sems.at[k]) for k, move in enumerate(moves)]
    for copy in copies:
        copy.start()
    for copy in copies:
        copy.wait()
    partial_velocity(
        [s_plane[c] for c in range(6)],
        [v_plane[c] for c in range(3)],
        time_step * b_plane[...],
        part_plane,
        (nothing, row_before),
    )
    partial_velocity(
        [s_rows[c] for c in range(6)],
        [v_rows[c] for c in range(3)],
        time_step * b_rows[...],
        part_rows,
        (row_before, nothing),
    )


def edges(stress, velocity, buoyancy, attenuation):
    _, nx, ny, nz = stress.shape
    return pl.pallas_call(
        edges_kernel,
        in_specs=[pl.BlockSpec(memory_space=pltpu.HBM)] * 4,
        out_shape=(
            f32(4, ny, nz),
            f32(4, nx, nz),
            f32(3, ny, nz),
            f32(3, nx, nz),
            f32(ny, nz),
            f32(nx, nz),
        ),
        scratch_shapes=[
            pltpu.VMEM((6, ny, nz), jnp.float32),
            pltpu.VMEM((6, nx, nz), jnp.float32),
            pltpu.VMEM((3, ny, nz), jnp.float32),
            pltpu.VMEM((3, nx, nz), jnp.float32),
            pltpu.SemaphoreType.DMA((13,)),
        ],
        compiler_params=pltpu.CompilerParams(vmem_limit_bytes=8 << 20),
        name="edges",
    )(*map(in_hbm, (stress, velocity, buoyancy, attenuation)))


def take_halo(part_plane, part_rows, b_plane, b_rows, plane, rows, out_plane, out_rows):
    factor_plane, factor_rows = time_step * b_plane[...], time_step * b_rows[...]
    for c in range(3):
        first_row = lax.broadcasted_iota(jnp.int32, factor_plane.shape, 0) == 0
        corner = jnp.where(first_row, rows[c, 0:1], 0.0)
        out_plane[c] = part_plane[c] - factor_plane * (plane[c] + corner)
        first_row = lax.broadcasted_iota(jnp.int32, factor_rows.shape, 0) == 0
        corner = jnp.where(first_row, plane[c, 0:1], 0.0)
        out_rows[c] = part_rows[c] - factor_rows * (rows[c] + corner)


def first_edges(part_plane, part_rows, b_plane, b_rows, plane, rows):
    return pl.pallas_call(
        take_halo,
        out_shape=(f32(*part_plane.shape), f32(*part_rows.shape)),
        compiler_params=pltpu.CompilerParams(vmem_limit_bytes=8 << 20),
        name="first_edges",
    )(part_plane, part_rows, b_plane, b_rows, plane, rows)


def sections_kernel(size_x, size_y, columns, planes, weight_y, weight_z, out, held):
    own = planes.shape[0]
    box_y, box_z = weight_y.shape[0], weight_z.shape[0]
    part = box_y // (columns * size_x)
    out[...] = jnp.zeros_like(out)
    held[...] = jnp.zeros_like(held)
    for t in range(own):
        partly = dot(weight_y[...], planes[t])
        held[t, strip : strip + box_y, :box_z] = dot(partly, weight_z[...], ((1,), (1,)))
    for k in range(columns):
        for i in range(size_x):
            start = strip + (k * size_x + i) * part - 1
            for t in range(own):
                piece = held[t, start : start + part + 1]
                row = t * (part + 1)
                out[i * size_y + size_y - columns + k, row : row + part + 1] = piece


def sections(planes, weight_y, weight_z, size_x, size_y, columns, height):
    own = planes.shape[0]
    return pl.pallas_call(
        functools.partial(sections_kernel, size_x, size_y, columns),
        out_shape=f32(size_x * size_y, height, lanes),
        scratch_shapes=[pltpu.VMEM((own, strip + weight_y.shape[0], lanes), jnp.float32)],
        compiler_params=pltpu.CompilerParams(vmem_limit_bytes=16 << 20),
        name="sections",
    )(planes, weight_y, weight_z)


def contract_kernel(own, part, nx, anchor, weight_x, gathered, out, padded):
    box_x, count = weight_x.shape
    size_x, height, _ = out.shape
    rows = height // (part + 1)
    devices = count // own
    stride = gathered.shape[0] // devices
    section = lax.broadcasted_iota(jnp.int32, (count, count), 0)
    column = lax.broadcasted_iota(jnp.int32, (count, count), 1)
    pick = section == own * lax.rem(column, devices) + lax.div(column, devices)
    weights = dot(weight_x[...], pick.astype(jnp.float32))
    padded[...] = jnp.zeros_like(padded)
    for r in range(part + 1):
        terms = [
            gathered[pl.ds(t * (part + 1) + r, devices, stride=stride), :] for t in range(own)
        ]
        box = dot(weights, jnp.concatenate(terms, 0))
        padded[r, pl.ds(anchor[0] + strip, box_x), :] = box
    for i in range(size_x):
        start = strip + i * nx
        for r in range(part + 1):
            out[i, r * rows : r * rows + nx] = padded[r, start : start + nx]
            out[i, r * rows + nx : (r + 1) * rows] = padded[r, start - 1 : start - 1 + rows - nx]


def contract(anchor, weight_x, gathered, own, part, nx, size_x, rows):
    return pl.pallas_call(
        functools.partial(contract_kernel, own, part, nx),
        in_specs=[
            pl.BlockSpec(memory_space=pltpu.SMEM),
            pl.BlockSpec(memory_space=pltpu.VMEM),
            pl.BlockSpec(memory_space=pltpu.VMEM),
        ],
        out_shape=f32(size_x, (part + 1) * rows, lanes),
        scratch_shapes=[pltpu.VMEM((part + 1, 2 * strip + size_x * nx, lanes), jnp.float32)],
        compiler_params=pltpu.CompilerParams(vmem_limit_bytes=16 << 20),
        name="contract",
    )(anchor, weight_x, gathered)


def place_kernel(part, *refs):
    anchor, box, cells, rate_plane, rate_rows = refs[:5]
    part_plane, part_rows, b_plane, b_rows, plane, rows = refs[5:11]
    out, out_plane, out_rows, first_plane, first_rows, held = refs[11:]
    size_x, height, _ = box.shape
    _, ny, nz = out.shape
    nx = out.shape[0] - 1
    span = height // (part + 1)
    for i in range(size_x):
        for r in range(part):
            y = i * part + r
            first = (r + 1) * span
            held[pl.ds(y, nx, stride=ny), :] = box[i, first : first + nx]
            held[nx * ny + y : nx * ny + y + 1] = box[i, first + nx : first + nx + 1]
    cell = lax.broadcasted_iota(jnp.int32, (lanes, nz), 1)
    which = lax.broadcasted_iota(jnp.int32, (lanes, nz), 0)
    pick = (cell - anchor[2] == which).astype(jnp.float32)

    def lost(values, rates):
        return (-time_step) * jnp.exp(-time_step * rates) * dot(values, pick)

    for t in range(0, nx, 4):
        values = (-time_step) * dot(held[t * ny : (t + 4) * ny], pick)
        for u in range(4):
            decay = jnp.exp(-time_step * cells[3, t + u])
            out[t + u + 1] = decay * values[u * ny : (u + 1) * ny]
    out[0] = jnp.zeros((ny, nz), jnp.float32)
    q_plane = lost(held[nx * ny :], rate_plane[3])
    q_rows = lost(box[0, 0:nx], rate_rows[3])
    out_plane[...] = q_plane
    out_rows[...] = q_rows
    take_halo(part_plane, part_rows, b_plane, b_rows, plane, rows, first_plane, first_rows)
    factor = time_step * b_plane[...]
    own = out[1]
    first_plane[0] = first_plane[0] + factor * (own - q_plane)
    first_plane[1] = first_plane[1] + factor * (own - after_row(own, q_rows[0:1]))
    first_plane[2] = first_plane[2] + factor * (own - shifted_up(own))
    factor = time_step * b_rows[...]
    own = out[1:, 0]
    first_rows[0] = first_rows[0] + factor * (own - after_row(own, q_plane[0:1]))
    first_rows[1] = first_rows[1] + factor * (own - q_rows)
    first_rows[2] = first_rows[2] + factor * (own - shifted_up(own))


def place(anchor, box, cells, rate_plane, rate_rows, halo, part):
    nx, ny, nz = cells.shape[1] - 1, *cells.shape[2:]
    on_chip = pl.BlockSpec(memory_space=pltpu.VMEM)
    return pl.pallas_call(
        functools.partial(place_kernel, part),
        in_specs=[pl.BlockSpec(memory_space=pltpu.SMEM)] + [on_chip] * (4 + len(halo)),
        out_specs=(on_chip,) * 5,
        out_shape=(
            pltpu.VMEM((nx + 1, ny, nz), jnp.float32),
            f32(ny, nz),
            f32(nx, nz),
            f32(3, ny, nz),
            f32(3, nx, nz),
        ),
        scratch_shapes=[pltpu.VMEM(((nx + 1) * ny, lanes), jnp.float32)],
        compiler_params=pltpu.CompilerParams(vmem_limit_bytes=12 << 20),
        name="place",
    )(anchor, box, in_vmem(cells), rate_plane, rate_rows, *halo)


def step_kernel(with_source, *refs):
    if with_source:
        source, plane, rows, upper_plane, upper_rows, source_plane, source_rows = refs[3:10]
        out_velocity, out_stress, stress, velocity = refs[10:14]
        cells, out_sems = refs[2], refs[14]
    else:
        fields, (plane, rows, upper_plane, upper_rows) = refs[:6], refs[6:10]
        stress, velocity, cells, last_plane, last_rows, part_plane, part_rows = refs[10:17]
        in_sems = refs[17]
    nx, ny, nz = cells.shape[1] - 1, *cells.shape[2:]
    chunks = nx // per

    def arriving(k):
        here, above = pl.ds(k * per, per), pl.ds(k * per + 1, per)
        moves = [
            (fields[0].at[:, here], stress.at[:, above]),
            (fields[1].at[:, here], velocity.at[:, here]),
        ]
        for n, field in enumerate(fields[2:6]):
            moves.append((field.at[here], cells.at[n, here]))
        return [pltpu.make_async_copy(*m, in_sems.at[k, n]) for n, m in enumerate(moves)]

    def leaving(k):
        here, above = pl.ds(k * per, per), pl.ds(k * per + 1, per)
        moves = [
            (velocity.at[:, here], out_velocity.at[:, here]),
            (stress.at[:, above], out_stress.at[:, here]),
        ]
        return [pltpu.make_async_copy(*m, out_sems.at[k, n]) for n, m in enumerate(moves)]

    def every(make, act):
        def one(n, _):
            for copy in make(chunks - 1 - n):
                act(copy)
            return 0

        lax.fori_loop(0, chunks, one, 0)

    if not with_source:
        every(arriving, lambda copy: copy.start())
    for c, which in enumerate((0, 3, 4)):
        stress[which, 0] = plane[c]
        velocity[c, nx] = upper_plane[c]
    if with_source:
        stress[0, 0] = plane[0] + source_plane[...]

    top = lax.broadcasted_iota(jnp.int32, (strip, nz), 0) == 0
    bottom = lax.broadcasted_iota(jnp.int32, (strip, nz), 0) == strip - 1

    def velocity_plane(x):
        above = [rows[c, pl.ds(x, 1)] for c in range(3)]
        if with_source:
            above[1] = above[1] + source_rows[pl.ds(x, 1)]
        above = [jnp.broadcast_to(row, (strip, nz)) for row in above]
        for r in range(ny // strip):
            here = slice(strip * r, strip * (r + 1))
            s = [stress[c, x + 1, here] for c in range(6)]
            before = [stress[c, x, here] for c in (0, 3, 4)]
            if with_source:
                extra = source[x + 1, here]
                s[:3] = [value + extra for value in s[:3]]
                before[0] = before[0] + source[x, here]
            s_xx, s_yy, s_zz, s_xy, s_xz, s_yz = s
            rolled = [pltpu.roll(value, 1, 0) for value in (s_xy, s_yy, s_yz)]
            up = [jnp.where(top, above[c], rolled[c]) for c in range(3)]
            factor = time_step * cells[0, x, here]
            sums = (
                (s_xx - before[0]) + (s_xy - up[0]) + (s_xz - shifted_up(s_xz)),
                (s_xy - before[1]) + (s_yy - up[1]) + (s_yz - shifted_up(s_yz)),
                (s_xz - before[2]) + (s_yz - up[2]) + (s_zz - shifted_up(s_zz)),
            )
            for c in range(3):
                velocity[c, x, here] = velocity[c, x, here] + factor * sums[c]
            above = rolled

    def stress_plane(x):
        below = [jnp.broadcast_to(upper_rows[c, pl.ds(x, 1)], (strip, nz)) for c in range(3)]
        for r in reversed(range(ny // strip)):
            here = slice(strip * r, strip * (r + 1))
            v = [velocity[c, x, here] for c in range(3)]
            rolled = [pltpu.roll(value, strip - 1, 0) for value in v]
            in_x = [velocity[c, x + 1, here] - v[c] for c in range(3)]
            in_y = [jnp.where(bottom, below[c], rolled[c]) - v[c] for c in range(3)]
            in_z = [shifted_down(v[c]) - v[c] for c in range(3)]
            decay = jnp.exp(-time_step * cells[3, x, here])
            shear = time_step * cells[2, x, here]
            normal = [in_x[0], in_y[1], in_z[2]]
            common = time_step * cells[1, x, here] * (normal[0] + normal[1] + normal[2])
            twice = 2.0 * shear
            if with_source:
                extra = source[x + 1, here]
                common = common + extra
            values = []
            for c in range(3):
                value = decay * (stress[c, x + 1, here] + (common + twice * normal[c]))
                values.append(value + extra if with_source else value)
            for c, (a, b) in enumerate(
                ((in_y[0], in_x[1]), (in_z[0], in_x[2]), (in_z[1], in_y[2])), 3
            ):
                values.append(decay * (stress[c, x + 1, here] + shear * (a + b)))
            for c in range(6):
                stress[c, x + 1, here] = values[c]
            if not with_source and r == ny // strip - 1:
                for c, which in enumerate((3, 1, 5)):
                    last_rows[c, pl.ds(x, 1)] = values[which][strip - 1 :]
            below = rolled

    def one_chunk(n, _):
        k = chunks - 1 - n

        if not with_source:

            @pl.when(k > 0)
            def _():
                for copy in arriving(k - 1):
                    copy.wait()

        def one_plane(m, _):
            x = k * per + (per - 1 - m)
            velocity_plane(x)
            stress_plane(x)
            return 0

        lax.fori_loop(0, per, one_plane, 0)
        if with_source:
            for copy in leaving(k):
                copy.start()
        return 0

    if not with_source:
        for copy in arriving(chunks - 1):
            copy.wait()
    lax.fori_loop(0, chunks, one_chunk, 0)
    if with_source:
        every(leaving, lambda copy: copy.wait())
    else:
        for c, which in enumerate((0, 3, 4)):
            last_plane[c] = stress[which, nx]
        partial_velocity(
            [stress[c, 1] for c in range(6)],
            [velocity[c, 0] for c in range(3)],
            time_step * cells[0, 0],
            part_plane,
            (nothing, row_before),
        )
        partial_velocity(
            [stress[c, 1:, 0] for c in range(6)],
            [velocity[c, :nx, 0] for c in range(3)],
            time_step * cells[0, :nx, 0],
            part_rows,
            (row_before, nothing),
        )


def estimate(nx, ny, nz, words):
    count = nx * ny * nz
    return pl.CostEstimate(
        flops=100 * count, bytes_accessed=4 * words * count, transcendentals=count
    )


def first_step(stress, velocity, coefficients, plane, rows, upper_plane, upper_rows):
    _, nx, ny, nz = velocity.shape
    fields = [in_hbm(a) for a in (stress, velocity, *coefficients)]
    on_chip = pl.BlockSpec(memory_space=pltpu.VMEM)
    return pl.pallas_call(
        functools.partial(step_kernel, False),
        in_specs=[pl.BlockSpec(memory_space=pltpu.HBM)] * len(fields) + [on_chip] * 4,
        out_specs=(on_chip,) * 7,
        out_shape=(
            *[pltpu.VMEM((n, nx + 1, ny, nz), jnp.float32) for n in (6, 3, 4)],
            *[f32(3, ny, nz), f32(3, nx, nz)] * 2,
        ),
        scratch_shapes=[pltpu.SemaphoreType.DMA((nx // per, len(fields)))],
        compiler_params=pltpu.CompilerParams(vmem_limit_bytes=20 << 20),
        cost_estimate=estimate(nx, ny, nz, 13),
        name="first_step",
    )(*fields, plane, rows, upper_plane, upper_rows)


def second_step(stress, velocity, cells, source, edges):
    _, nx, ny, nz = cells.shape
    nx = nx - 1
    held = [in_vmem(a) for a in (stress, velocity, cells, source)]
    on_chip = pl.BlockSpec(memory_space=pltpu.VMEM)
    out = pl.pallas_call(
        functools.partial(step_kernel, True),
        in_specs=[on_chip] * (len(held) + len(edges)),
        out_specs=(pl.BlockSpec(memory_space=pltpu.HBM),) * 2 + (on_chip,) * 2,
        out_shape=(
            *[pltpu.HBM((n, nx, ny, nz), jnp.float32) for n in (3, 6)],
            *[pltpu.VMEM(a.shape, jnp.float32) for a in (stress, velocity)],
        ),
        input_output_aliases={0: 2, 1: 3},
        scratch_shapes=[pltpu.SemaphoreType.DMA((nx // per, 2))],
        compiler_params=pltpu.CompilerParams(vmem_limit_bytes=20 << 20),
        cost_estimate=estimate(nx, ny, nz, 9),
        name="second_step",
    )(*held, *edges)
    return out[0], out[1]


def shards(
    source_planes,
    weight_x,
    weight_y,
    weight_z,
    box_anchor,
    velocity,
    stress,
    lame_lambda,
    lame_mu,
    buoyancy,
    attenuation,
):
    nx, ny, nz = lame_mu.shape
    box_x, sources = weight_x.shape
    box_y = weight_y.shape[0]
    size_x, size_y = lax.axis_size("gx"), lax.axis_size("gy")
    own = source_planes.shape[0]
    columns = box_y // ny
    part = ny // size_x
    height = -(-own * (part + 1) // strip) * strip
    coefficients = (buoyancy, lame_lambda, lame_mu, attenuation)

    pieces = sections(source_planes, weight_y, weight_z, size_x, size_y, columns, height)
    gathered = lax.all_to_all(pieces, ("gx", "gy"), 0, 0, tiled=True)
    send_x, send_y, *parts = edges(stress, velocity, buoyancy, attenuation)
    plane = neighbour(send_x, "gx", 1)
    rows = neighbour(send_y, "gy", 1)
    first_x, first_y = first_edges(*parts, plane, rows)

    gathered, first_x, first_y = lax.optimization_barrier((gathered, first_x, first_y))
    gathered = gathered.reshape(size_x * size_y * height, lanes)
    shares = contract(box_anchor, weight_x, gathered, own, part, nx, size_x, nx + strip)
    shares, first_x, first_y = lax.optimization_barrier((shares, first_x, first_y))
    box = lax.all_to_all(shares, "gx", 0, 0, tiled=True)
    upper_x = neighbour(first_x, "gx", -1)
    upper_y = neighbour(first_y, "gy", -1)
    box, upper_x, upper_y = lax.optimization_barrier((box, upper_x, upper_y))

    strained, speed, cells, last_x, last_y, *parts[:2] = first_step(
        stress, velocity, coefficients, plane, rows, upper_x, upper_y
    )
    lower_x = neighbour(last_x, "gx", 1)
    lower_y = neighbour(last_y, "gy", 1)
    halo = (*parts, lower_x, lower_y)
    *source, first_x, first_y = place(box_anchor, box, cells, plane, rows, halo, part)
    upper_x = neighbour(first_x, "gx", -1)
    upper_y = neighbour(first_y, "gy", -1)
    moved = (lower_x, lower_y, upper_x, upper_y, *source[1:])
    return second_step(strained, speed, cells, source[0], moved)


def solution(mesh):
    in_specs = (
        P(("gx", "gy"), None, None),
        P(),
        P(),
        P(),
        P(),
        P(None, "gx", "gy", None),
        P(None, "gx", "gy", None),
        P("gx", "gy", None),
        P("gx", "gy", None),
        P("gx", "gy", None),
        P("gx", "gy", None),
    )
    out_specs = (P(None, "gx", "gy", None), P(None, "gx", "gy", None))
    return jax.shard_map(shards, mesh=mesh, in_specs=in_specs, out_specs=out_specs, check_vma=False)
```

```python
import functools

import jax
import jax.numpy as jnp
from jax import lax
from jax.experimental import pallas as pl
from jax.experimental.pallas import tpu as pltpu
from jax.sharding import PartitionSpec as P

time_step = 0.2
precise = lax.Precision.HIGHEST
strip = 8
lanes = 128
per = 3


def neighbour(value, axis, by):
    size = lax.axis_size(axis)
    pairs = [(i, i + by) for i in range(size) if 0 <= i + by < size]
    return lax.ppermute(value, axis, pairs)


def in_hbm(value):
    return pltpu.with_memory_space_constraint(value, pltpu.HBM)


def in_vmem(value):
    return pltpu.with_memory_space_constraint(value, pltpu.VMEM)


def f32(*shape):
    return jax.ShapeDtypeStruct(shape, jnp.float32)


def dot(a, b, contract=((1,), (0,))):
    return lax.dot_general(
        a, b, (contract, ((), ())), precision=precise, preferred_element_type=jnp.float32
    )


def shifted_up(values):
    first = jnp.zeros((values.shape[0], 1), jnp.float32)
    return jnp.concatenate([first, values[:, :-1]], 1)


def shifted_down(values):
    last = jnp.zeros((values.shape[0], 1), jnp.float32)
    return jnp.concatenate([values[:, 1:], last], 1)


def after_row(values, row):
    where = lax.broadcasted_iota(jnp.int32, values.shape, 0)
    return jnp.where(where == 0, row, pltpu.roll(values, 1, 0))


def partial_velocity(stress, velocity, factor, out, before):
    xx, yy, zz, xy, xz, yz = stress
    along_x, along_y = before
    out[0] = velocity[0] + factor * (
        (xx - along_x(xx)) + (xy - along_y(xy)) + (xz - shifted_up(xz))
    )
    out[1] = velocity[1] + factor * (
        (xy - along_x(xy)) + (yy - along_y(yy)) + (yz - shifted_up(yz))
    )
    out[2] = velocity[2] + factor * (
        (xz - along_x(xz)) + (yz - along_y(yz)) + (zz - shifted_up(zz))
    )


def nothing(values):
    return jnp.zeros_like(values)


def row_before(values):
    return after_row(values, 0.0)


def edges_kernel(stress, velocity, buoyancy, attenuation, *refs):
    out_plane, out_rows, part_plane, part_rows, b_plane, b_rows = refs[:6]
    s_plane, s_rows, v_plane, v_rows, sems = refs[6:]
    _, nx, ny, _ = stress.shape
    moves = [
        (stress.at[:, 0], s_plane),
        (stress.at[:, :, 0], s_rows),
        (velocity.at[:, 0], v_plane),
        (velocity.at[:, :, 0], v_rows),
        (buoyancy.at[0], b_plane),
        (buoyancy.at[:, 0], b_rows),
        (stress.at[0, nx - 1], out_plane.at[0]),
        (stress.at[3:5, nx - 1], out_plane.at[1:3]),
        (attenuation.at[nx - 1], out_plane.at[3]),
        (stress.at[3, :, ny - 1], out_rows.at[0]),
        (stress.at[1, :, ny - 1], out_rows.at[1]),
        (stress.at[5, :, ny - 1], out_rows.at[2]),
        (attenuation.at[:, ny - 1], out_rows.at[3]),
    ]
    copies = [pltpu.make_async_copy(*move, sems.at[k]) for k, move in enumerate(moves)]
    for copy in copies:
        copy.start()
    for copy in copies:
        copy.wait()
    partial_velocity(
        [s_plane[c] for c in range(6)],
        [v_plane[c] for c in range(3)],
        time_step * b_plane[...],
        part_plane,
        (nothing, row_before),
    )
    partial_velocity(
        [s_rows[c] for c in range(6)],
        [v_rows[c] for c in range(3)],
        time_step * b_rows[...],
        part_rows,
        (row_before, nothing),
    )


def edges(stress, velocity, buoyancy, attenuation):
    _, nx, ny, nz = stress.shape
    return pl.pallas_call(
        edges_kernel,
        in_specs=[pl.BlockSpec(memory_space=pltpu.HBM)] * 4,
        out_shape=(
            f32(4, ny, nz),
            f32(4, nx, nz),
            f32(3, ny, nz),
            f32(3, nx, nz),
            f32(ny, nz),
            f32(nx, nz),
        ),
        scratch_shapes=[
            pltpu.VMEM((6, ny, nz), jnp.float32),
            pltpu.VMEM((6, nx, nz), jnp.float32),
            pltpu.VMEM((3, ny, nz), jnp.float32),
            pltpu.VMEM((3, nx, nz), jnp.float32),
            pltpu.SemaphoreType.DMA((13,)),
        ],
        compiler_params=pltpu.CompilerParams(vmem_limit_bytes=8 << 20),
        name="edges",
    )(*map(in_hbm, (stress, velocity, buoyancy, attenuation)))


def take_halo(part_plane, part_rows, b_plane, b_rows, plane, rows, out_plane, out_rows):
    factor_plane, factor_rows = time_step * b_plane[...], time_step * b_rows[...]
    for c in range(3):
        first_row = lax.broadcasted_iota(jnp.int32, factor_plane.shape, 0) == 0
        corner = jnp.where(first_row, rows[c, 0:1], 0.0)
        out_plane[c] = part_plane[c] - factor_plane * (plane[c] + corner)
        first_row = lax.broadcasted_iota(jnp.int32, factor_rows.shape, 0) == 0
        corner = jnp.where(first_row, plane[c, 0:1], 0.0)
        out_rows[c] = part_rows[c] - factor_rows * (rows[c] + corner)


def first_edges(part_plane, part_rows, b_plane, b_rows, plane, rows):
    return pl.pallas_call(
        take_halo,
        out_shape=(f32(*part_plane.shape), f32(*part_rows.shape)),
        compiler_params=pltpu.CompilerParams(vmem_limit_bytes=8 << 20),
        name="first_edges",
    )(part_plane, part_rows, b_plane, b_rows, plane, rows)


def sections_kernel(size_x, size_y, columns, planes, weight_y, weight_z, out, *refs):
    held, planes_in, y_in, z_in, sems = refs
    own = planes.shape[0]
    box_y, box_z = weight_y.shape[0], weight_z.shape[0]
    part = box_y // (columns * size_x)
    moves = [(weight_y, y_in), (weight_z, z_in)]
    moves += [(planes.at[t], planes_in.at[t]) for t in range(own)]
    copies = [pltpu.make_async_copy(*move, sems.at[k]) for k, move in enumerate(moves)]
    for copy in copies:
        copy.start()
    out[...] = jnp.zeros_like(out)
    held[...] = jnp.zeros_like(held)
    copies[0].wait()
    copies[1].wait()
    for t in range(own):
        copies[2 + t].wait()
        partly = dot(y_in[...], planes_in[t])
        held[t, strip : strip + box_y, :box_z] = dot(partly, z_in[...], ((1,), (1,)))
    for k in range(columns):
        for i in range(size_x):
            start = strip + (k * size_x + i) * part - 1
            for t in range(own):
                piece = held[t, start : start + part + 1]
                row = t * (part + 1)
                out[i * size_y + size_y - columns + k, row : row + part + 1] = piece


def sections(planes, weight_y, weight_z, size_x, size_y, columns, height):
    own, box_y = planes.shape[0], weight_y.shape[0]
    return pl.pallas_call(
        functools.partial(sections_kernel, size_x, size_y, columns),
        in_specs=[pl.BlockSpec(memory_space=pltpu.HBM)] * 3,
        out_shape=f32(size_x * size_y, height, lanes),
        scratch_shapes=[
            pltpu.VMEM((own, strip + box_y, lanes), jnp.float32),
            *[pltpu.VMEM(a.shape, jnp.float32) for a in (planes, weight_y, weight_z)],
            pltpu.SemaphoreType.DMA((2 + own,)),
        ],
        compiler_params=pltpu.CompilerParams(vmem_limit_bytes=16 << 20),
        name="sections",
    )(*map(in_hbm, (planes, weight_y, weight_z)))


def contract_kernel(own, part, nx, anchor, weight_x, gathered, out, padded):
    box_x, count = weight_x.shape
    size_x, height, _ = out.shape
    rows = height // (part + 1)
    devices = count // own
    stride = gathered.shape[0] // devices
    section = lax.broadcasted_iota(jnp.int32, (count, count), 0)
    column = lax.broadcasted_iota(jnp.int32, (count, count), 1)
    pick = section == own * lax.rem(column, devices) + lax.div(column, devices)
    weights = dot(weight_x[...], pick.astype(jnp.float32))
    padded[...] = jnp.zeros_like(padded)
    for r in range(part + 1):
        terms = [
            gathered[pl.ds(t * (part + 1) + r, devices, stride=stride), :] for t in range(own)
        ]
        box = dot(weights, jnp.concatenate(terms, 0))
        padded[r, pl.ds(anchor[0] + strip, box_x), :] = box
    for i in range(size_x):
        start = strip + i * nx
        for r in range(part + 1):
            out[i, r * rows : r * rows + nx] = padded[r, start : start + nx]
            out[i, r * rows + nx : (r + 1) * rows] = padded[r, start - 1 : start - 1 + rows - nx]


def contract(anchor, weight_x, gathered, own, part, nx, size_x, rows):
    return pl.pallas_call(
        functools.partial(contract_kernel, own, part, nx),
        in_specs=[
            pl.BlockSpec(memory_space=pltpu.SMEM),
            pl.BlockSpec(memory_space=pltpu.VMEM),
            pl.BlockSpec(memory_space=pltpu.VMEM),
        ],
        out_shape=f32(size_x, (part + 1) * rows, lanes),
        scratch_shapes=[pltpu.VMEM((part + 1, 2 * strip + size_x * nx, lanes), jnp.float32)],
        compiler_params=pltpu.CompilerParams(vmem_limit_bytes=16 << 20),
        name="contract",
    )(anchor, weight_x, gathered)


def place_kernel(part, anchor, box, cells, rate_plane, rate_rows, *refs):
    out, out_plane, out_rows, held = refs
    size_x, height, _ = box.shape
    _, ny, nz = out.shape
    nx = out.shape[0] - 1
    span = height // (part + 1)
    for i in range(size_x):
        for r in range(part):
            y = i * part + r
            first = (r + 1) * span
            held[pl.ds(y, nx, stride=ny), :] = box[i, first : first + nx]
            held[nx * ny + y : nx * ny + y + 1] = box[i, first + nx : first + nx + 1]
    cell = lax.broadcasted_iota(jnp.int32, (lanes, nz), 1)
    which = lax.broadcasted_iota(jnp.int32, (lanes, nz), 0)
    pick = (cell - anchor[2] == which).astype(jnp.float32)

    def lost(values, rates):
        return (-time_step) * jnp.exp(-time_step * rates) * dot(values, pick)

    for t in range(0, nx, 4):
        values = (-time_step) * dot(held[t * ny : (t + 4) * ny], pick)
        for u in range(4):
            decay = jnp.exp(-time_step * cells[3, t + u])
            out[t + u + 1] = decay * values[u * ny : (u + 1) * ny]
    out[0] = jnp.zeros((ny, nz), jnp.float32)
    out_plane[...] = lost(held[nx * ny :], rate_plane[3])
    out_rows[...] = lost(box[0, 0:nx], rate_rows[3])


def place(anchor, box, cells, rate_plane, rate_rows, part):
    nx, ny, nz = cells.shape[1] - 1, *cells.shape[2:]
    on_chip = pl.BlockSpec(memory_space=pltpu.VMEM)
    return pl.pallas_call(
        functools.partial(place_kernel, part),
        in_specs=[pl.BlockSpec(memory_space=pltpu.SMEM)] + [on_chip] * 4,
        out_specs=(on_chip,) * 3,
        out_shape=(pltpu.VMEM((nx + 1, ny, nz), jnp.float32), f32(ny, nz), f32(nx, nz)),
        scratch_shapes=[pltpu.VMEM(((nx + 1) * ny, lanes), jnp.float32)],
        compiler_params=pltpu.CompilerParams(vmem_limit_bytes=12 << 20),
        name="place",
    )(anchor, box, in_vmem(cells), rate_plane, rate_rows)


def second_edges_kernel(*refs):
    part_plane, part_rows, b_plane, b_rows, plane, rows = refs[:6]
    source, source_plane, source_rows, first_plane, first_rows = refs[6:]
    take_halo(part_plane, part_rows, b_plane, b_rows, plane, rows, first_plane, first_rows)
    q_plane, q_rows = source_plane[...], source_rows[...]
    factor = time_step * b_plane[...]
    own = source[1]
    first_plane[0] = first_plane[0] + factor * (own - q_plane)
    first_plane[1] = first_plane[1] + factor * (own - after_row(own, q_rows[0:1]))
    first_plane[2] = first_plane[2] + factor * (own - shifted_up(own))
    factor = time_step * b_rows[...]
    own = source[1:, 0]
    first_rows[0] = first_rows[0] + factor * (own - after_row(own, q_plane[0:1]))
    first_rows[1] = first_rows[1] + factor * (own - q_rows)
    first_rows[2] = first_rows[2] + factor * (own - shifted_up(own))


def second_edges(parts, plane, rows, source):
    on_chip = pl.BlockSpec(memory_space=pltpu.VMEM)
    return pl.pallas_call(
        second_edges_kernel,
        in_specs=[on_chip] * 9,
        out_specs=(on_chip,) * 2,
        out_shape=(f32(*parts[0].shape), f32(*parts[1].shape)),
        compiler_params=pltpu.CompilerParams(vmem_limit_bytes=8 << 20),
        name="second_edges",
    )(*parts, plane, rows, in_vmem(source[0]), *source[1:])


def step_kernel(kind, *refs):
    with_source = kind != "first"
    if kind == "velocity":
        cells, source, plane, rows, source_plane, source_rows = refs[2:8]
        out_velocity, stress, velocity, out_sems = refs[8:]
    elif kind == "stress":
        cells, source, upper_plane, upper_rows = refs[2:6]
        out_stress, stress, velocity, out_sems = refs[6:]
    else:
        fields, (plane, rows, upper_plane, upper_rows) = refs[:6], refs[6:10]
        stress, velocity, cells, last_plane, last_rows, part_plane, part_rows = refs[10:17]
        in_sems = refs[17]
    nx, ny, nz = cells.shape[1] - 1, *cells.shape[2:]
    chunks = nx // per

    def arriving(k):
        here, above = pl.ds(k * per, per), pl.ds(k * per + 1, per)
        moves = [
            (fields[0].at[:, here], stress.at[:, above]),
            (fields[1].at[:, here], velocity.at[:, here]),
        ]
        for n, field in enumerate(fields[2:6]):
            moves.append((field.at[here], cells.at[n, here]))
        return [pltpu.make_async_copy(*m, in_sems.at[k, n]) for n, m in enumerate(moves)]

    def leaving(k):
        here, above = pl.ds(k * per, per), pl.ds(k * per + 1, per)
        if kind == "velocity":
            move = (velocity.at[:, here], out_velocity.at[:, here])
        else:
            move = (stress.at[:, above], out_stress.at[:, here])
        return [pltpu.make_async_copy(*move, out_sems.at[k])]

    def every(make, act):
        def one(n, _):
            for copy in make(chunks - 1 - n):
                act(copy)
            return 0

        lax.fori_loop(0, chunks, one, 0)

    if not with_source:
        every(arriving, lambda copy: copy.start())
    if kind != "stress":
        for c, which in enumerate((0, 3, 4)):
            stress[which, 0] = plane[c]
        if with_source:
            stress[0, 0] = plane[0] + source_plane[...]
    if kind != "velocity":
        for c in range(3):
            velocity[c, nx] = upper_plane[c]

    top = lax.broadcasted_iota(jnp.int32, (strip, nz), 0) == 0
    bottom = lax.broadcasted_iota(jnp.int32, (strip, nz), 0) == strip - 1

    def velocity_plane(x):
        above = [rows[c, pl.ds(x, 1)] for c in range(3)]
        if with_source:
            above[1] = above[1] + source_rows[pl.ds(x, 1)]
        above = [jnp.broadcast_to(row, (strip, nz)) for row in above]
        for r in range(ny // strip):
            here = slice(strip * r, strip * (r + 1))
            s = [stress[c, x + 1, here] for c in range(6)]
            before = [stress[c, x, here] for c in (0, 3, 4)]
            if with_source:
                extra = source[x + 1, here]
                s[:3] = [value + extra for value in s[:3]]
                before[0] = before[0] + source[x, here]
            s_xx, s_yy, s_zz, s_xy, s_xz, s_yz = s
            rolled = [pltpu.roll(value, 1, 0) for value in (s_xy, s_yy, s_yz)]
            up = [jnp.where(top, above[c], rolled[c]) for c in range(3)]
            factor = time_step * cells[0, x, here]
            sums = (
                (s_xx - before[0]) + (s_xy - up[0]) + (s_xz - shifted_up(s_xz)),
                (s_xy - before[1]) + (s_yy - up[1]) + (s_yz - shifted_up(s_yz)),
                (s_xz - before[2]) + (s_yz - up[2]) + (s_zz - shifted_up(s_zz)),
            )
            for c in range(3):
                velocity[c, x, here] = velocity[c, x, here] + factor * sums[c]
            above = rolled

    def stress_plane(x):
        below = [jnp.broadcast_to(upper_rows[c, pl.ds(x, 1)], (strip, nz)) for c in range(3)]
        for r in reversed(range(ny // strip)):
            here = slice(strip * r, strip * (r + 1))
            v = [velocity[c, x, here] for c in range(3)]
            rolled = [pltpu.roll(value, strip - 1, 0) for value in v]
            in_x = [velocity[c, x + 1, here] - v[c] for c in range(3)]
            in_y = [jnp.where(bottom, below[c], rolled[c]) - v[c] for c in range(3)]
            in_z = [shifted_down(v[c]) - v[c] for c in range(3)]
            decay = jnp.exp(-time_step * cells[3, x, here])
            shear = time_step * cells[2, x, here]
            normal = [in_x[0], in_y[1], in_z[2]]
            common = time_step * cells[1, x, here] * (normal[0] + normal[1] + normal[2])
            twice = 2.0 * shear
            if with_source:
                extra = source[x + 1, here]
                common = common + extra
            values = []
            for c in range(3):
                value = decay * (stress[c, x + 1, here] + (common + twice * normal[c]))
                values.append(value + extra if with_source else value)
            for c, (a, b) in enumerate(
                ((in_y[0], in_x[1]), (in_z[0], in_x[2]), (in_z[1], in_y[2])), 3
            ):
                values.append(decay * (stress[c, x + 1, here] + shear * (a + b)))
            for c in range(6):
                stress[c, x + 1, here] = values[c]
            if not with_source and r == ny // strip - 1:
                for c, which in enumerate((3, 1, 5)):
                    last_rows[c, pl.ds(x, 1)] = values[which][strip - 1 :]
            below = rolled

    def one_chunk(n, _):
        k = chunks - 1 - n

        if not with_source:

            @pl.when(k > 0)
            def _():
                for copy in arriving(k - 1):
                    copy.wait()

        def one_plane(m, _):
            x = k * per + (per - 1 - m)
            if kind != "stress":
                velocity_plane(x)
            if kind != "velocity":
                stress_plane(x)
            return 0

        lax.fori_loop(0, per, one_plane, 0)
        if with_source:
            for copy in leaving(k):
                copy.start()
        return 0

    if not with_source:
        for copy in arriving(chunks - 1):
            copy.wait()
    lax.fori_loop(0, chunks, one_chunk, 0)
    if with_source:
        every(leaving, lambda copy: copy.wait())
    else:
        for c, which in enumerate((0, 3, 4)):
            last_plane[c] = stress[which, nx]
        partial_velocity(
            [stress[c, 1] for c in range(6)],
            [velocity[c, 0] for c in range(3)],
            time_step * cells[0, 0],
            part_plane,
            (nothing, row_before),
        )
        partial_velocity(
            [stress[c, 1:, 0] for c in range(6)],
            [velocity[c, :nx, 0] for c in range(3)],
            time_step * cells[0, :nx, 0],
            part_rows,
            (row_before, nothing),
        )


def estimate(nx, ny, nz, words):
    count = nx * ny * nz
    return pl.CostEstimate(
        flops=100 * count, bytes_accessed=4 * words * count, transcendentals=count
    )


def first_step(stress, velocity, coefficients, plane, rows, upper_plane, upper_rows):
    _, nx, ny, nz = velocity.shape
    fields = [in_hbm(a) for a in (stress, velocity, *coefficients)]
    on_chip = pl.BlockSpec(memory_space=pltpu.VMEM)
    return pl.pallas_call(
        functools.partial(step_kernel, "first"),
        in_specs=[pl.BlockSpec(memory_space=pltpu.HBM)] * len(fields) + [on_chip] * 4,
        out_specs=(on_chip,) * 7,
        out_shape=(
            *[pltpu.VMEM((n, nx + 1, ny, nz), jnp.float32) for n in (6, 3, 4)],
            *[f32(3, ny, nz), f32(3, nx, nz)] * 2,
        ),
        scratch_shapes=[pltpu.SemaphoreType.DMA((nx // per, len(fields)))],
        compiler_params=pltpu.CompilerParams(vmem_limit_bytes=20 << 20),
        cost_estimate=estimate(nx, ny, nz, 13),
        name="first_step",
    )(*fields, plane, rows, upper_plane, upper_rows)


def second_step(kind, stress, velocity, cells, source, edges):
    nx, ny, nz = cells.shape[1] - 1, *cells.shape[2:]
    held = [in_vmem(a) for a in (stress, velocity, cells, source)]
    on_chip = pl.BlockSpec(memory_space=pltpu.VMEM)
    parts = 3 if kind == "velocity" else 6
    return pl.pallas_call(
        functools.partial(step_kernel, kind),
        in_specs=[on_chip] * (len(held) + len(edges)),
        out_specs=(pl.BlockSpec(memory_space=pltpu.HBM), on_chip, on_chip),
        out_shape=(
            pltpu.HBM((parts, nx, ny, nz), jnp.float32),
            *[pltpu.VMEM(a.shape, jnp.float32) for a in (stress, velocity)],
        ),
        input_output_aliases={0: 1, 1: 2},
        scratch_shapes=[pltpu.SemaphoreType.DMA((nx // per,))],
        compiler_params=pltpu.CompilerParams(vmem_limit_bytes=20 << 20),
        cost_estimate=estimate(nx, ny, nz, parts),
        name="second_" + kind,
    )(*held, *edges)


def shards(
    source_planes,
    weight_x,
    weight_y,
    weight_z,
    box_anchor,
    velocity,
    stress,
    lame_lambda,
    lame_mu,
    buoyancy,
    attenuation,
):
    nx, ny, nz = lame_mu.shape
    box_x, sources = weight_x.shape
    box_y = weight_y.shape[0]
    size_x, size_y = lax.axis_size("gx"), lax.axis_size("gy")
    own = source_planes.shape[0]
    columns = box_y // ny
    part = ny // size_x
    height = -(-own * (part + 1) // strip) * strip
    coefficients = (buoyancy, lame_lambda, lame_mu, attenuation)

    pieces = sections(source_planes, weight_y, weight_z, size_x, size_y, columns, height)
    gathered = lax.all_to_all(pieces, ("gx", "gy"), 0, 0, tiled=True)
    send_x, send_y, *parts = edges(stress, velocity, buoyancy, attenuation)
    plane = neighbour(send_x, "gx", 1)
    rows = neighbour(send_y, "gy", 1)
    first_x, first_y = first_edges(*parts, plane, rows)

    gathered, first_x, first_y = lax.optimization_barrier((gathered, first_x, first_y))
    gathered = gathered.reshape(size_x * size_y * height, lanes)
    shares = contract(box_anchor, weight_x, gathered, own, part, nx, size_x, nx + strip)
    shares, first_x, first_y = lax.optimization_barrier((shares, first_x, first_y))
    box = lax.all_to_all(shares, "gx", 0, 0, tiled=True)
    upper_x = neighbour(first_x, "gx", -1)
    upper_y = neighbour(first_y, "gy", -1)
    box, upper_x, upper_y = lax.optimization_barrier((box, upper_x, upper_y))

    strained, speed, cells, last_x, last_y, *parts[:2] = first_step(
        stress, velocity, coefficients, plane, rows, upper_x, upper_y
    )
    lower_x = neighbour(last_x, "gx", 1)
    lower_y = neighbour(last_y, "gy", 1)
    source = place(box_anchor, box, cells, plane, rows, part)
    first_x, first_y = second_edges(parts, lower_x, lower_y, source)
    upper_x = neighbour(first_x, "gx", -1)
    upper_y = neighbour(first_y, "gy", -1)
    velocity_out, strained, speed = second_step(
        "velocity", strained, speed, cells, source[0], (lower_x, lower_y, *source[1:])
    )
    stress_out, _, _ = second_step(
        "stress", strained, speed, cells, source[0], (upper_x, upper_y)
    )
    return (velocity_out, stress_out)


def solution(mesh):
    in_specs = (
        P(("gx", "gy"), None, None),
        P(),
        P(),
        P(),
        P(),
        P(None, "gx", "gy", None),
        P(None, "gx", "gy", None),
        P("gx", "gy", None),
        P("gx", "gy", None),
        P("gx", "gy", None),
        P("gx", "gy", None),
    )
    out_specs = (P(None, "gx", "gy", None), P(None, "gx", "gy", None))
    return jax.shard_map(shards, mesh=mesh, in_specs=in_specs, out_specs=out_specs, check_vma=False)
```

```python
import functools

import jax
import jax.numpy as jnp
from jax import lax
from jax.experimental import pallas as pl
from jax.experimental.pallas import tpu as pltpu
from jax.sharding import PartitionSpec as P

time_step = 0.2
strip = 8
lanes = 128
per = 3


def neighbour(value, axis, by):
    size = lax.axis_size(axis)
    pairs = [(i, i + by) for i in range(size) if 0 <= i + by < size]
    return lax.ppermute(value, axis, pairs)


def in_hbm(value):
    return pltpu.with_memory_space_constraint(value, pltpu.HBM)


def in_vmem(value):
    return pltpu.with_memory_space_constraint(value, pltpu.VMEM)


def f32(*shape):
    return jax.ShapeDtypeStruct(shape, jnp.float32)


def split(values, parts=2):
    out = []
    for _ in range(parts):
        out.append(values.astype(jnp.bfloat16))
        values = values - out[-1].astype(jnp.float32)
    return out


def dot(a, b, contract=((1,), (0,))):
    return sum(
        lax.dot_general(
            a[i], b[j], (contract, ((), ())), preferred_element_type=jnp.float32
        )
        for i, j in sorted(
            ((i, j) for i in range(len(a)) for j in range(len(b))), key=lambda ij: -sum(ij)
        )
        if i + j < max(len(a), len(b))
    )


def shifted_up(values):
    first = jnp.zeros((values.shape[0], 1), jnp.float32)
    return jnp.concatenate([first, values[:, :-1]], 1)


def shifted_down(values):
    last = jnp.zeros((values.shape[0], 1), jnp.float32)
    return jnp.concatenate([values[:, 1:], last], 1)


def after_row(values, row):
    where = lax.broadcasted_iota(jnp.int32, values.shape, 0)
    return jnp.where(where == 0, row, pltpu.roll(values, 1, 0))


def partial_velocity(stress, velocity, factor, out, before):
    xx, yy, zz, xy, xz, yz = stress
    along_x, along_y = before
    out[0] = velocity[0] + factor * (
        (xx - along_x(xx)) + (xy - along_y(xy)) + (xz - shifted_up(xz))
    )
    out[1] = velocity[1] + factor * (
        (xy - along_x(xy)) + (yy - along_y(yy)) + (yz - shifted_up(yz))
    )
    out[2] = velocity[2] + factor * (
        (xz - along_x(xz)) + (yz - along_y(yz)) + (zz - shifted_up(zz))
    )


def nothing(values):
    return jnp.zeros_like(values)


def row_before(values):
    return after_row(values, 0.0)


def edges_kernel(stress, velocity, buoyancy, attenuation, *refs):
    out_plane, out_rows, part_plane, part_rows, b_plane, b_rows = refs[:6]
    s_plane, s_rows, v_plane, v_rows, sems = refs[6:]
    _, nx, ny, _ = stress.shape
    moves = [
        (stress.at[:, 0], s_plane),
        (stress.at[:, :, 0], s_rows),
        (velocity.at[:, 0], v_plane),
        (velocity.at[:, :, 0], v_rows),
        (buoyancy.at[0], b_plane),
        (buoyancy.at[:, 0], b_rows),
        (stress.at[0, nx - 1], out_plane.at[0]),
        (stress.at[3:5, nx - 1], out_plane.at[1:3]),
        (attenuation.at[nx - 1], out_plane.at[3]),
        (stress.at[3, :, ny - 1], out_rows.at[0]),
        (stress.at[1, :, ny - 1], out_rows.at[1]),
        (stress.at[5, :, ny - 1], out_rows.at[2]),
        (attenuation.at[:, ny - 1], out_rows.at[3]),
    ]
    copies = [pltpu.make_async_copy(*move, sems.at[k]) for k, move in enumerate(moves)]
    for copy in copies:
        copy.start()
    for copy in copies:
        copy.wait()
    partial_velocity(
        [s_plane[c] for c in range(6)],
        [v_plane[c] for c in range(3)],
        time_step * b_plane[...],
        part_plane,
        (nothing, row_before),
    )
    partial_velocity(
        [s_rows[c] for c in range(6)],
        [v_rows[c] for c in range(3)],
        time_step * b_rows[...],
        part_rows,
        (row_before, nothing),
    )


def edges(stress, velocity, buoyancy, attenuation):
    _, nx, ny, nz = stress.shape
    return pl.pallas_call(
        edges_kernel,
        in_specs=[pl.BlockSpec(memory_space=pltpu.HBM)] * 4,
        out_shape=(
            f32(4, ny, nz),
            f32(4, nx, nz),
            f32(3, ny, nz),
            f32(3, nx, nz),
            f32(ny, nz),
            f32(nx, nz),
        ),
        scratch_shapes=[
            pltpu.VMEM((6, ny, nz), jnp.float32),
            pltpu.VMEM((6, nx, nz), jnp.float32),
            pltpu.VMEM((3, ny, nz), jnp.float32),
            pltpu.VMEM((3, nx, nz), jnp.float32),
            pltpu.SemaphoreType.DMA((13,)),
        ],
        compiler_params=pltpu.CompilerParams(vmem_limit_bytes=8 << 20),
        name="edges",
    )(*map(in_hbm, (stress, velocity, buoyancy, attenuation)))


def take_halo(part_plane, part_rows, b_plane, b_rows, plane, rows, out_plane, out_rows):
    factor_plane, factor_rows = time_step * b_plane[...], time_step * b_rows[...]
    for c in range(3):
        first_row = lax.broadcasted_iota(jnp.int32, factor_plane.shape, 0) == 0
        corner = jnp.where(first_row, rows[c, 0:1], 0.0)
        out_plane[c] = part_plane[c] - factor_plane * (plane[c] + corner)
        first_row = lax.broadcasted_iota(jnp.int32, factor_rows.shape, 0) == 0
        corner = jnp.where(first_row, plane[c, 0:1], 0.0)
        out_rows[c] = part_rows[c] - factor_rows * (rows[c] + corner)


def first_edges(part_plane, part_rows, b_plane, b_rows, plane, rows):
    return pl.pallas_call(
        take_halo,
        out_shape=(f32(*part_plane.shape), f32(*part_rows.shape)),
        compiler_params=pltpu.CompilerParams(vmem_limit_bytes=8 << 20),
        name="first_edges",
    )(part_plane, part_rows, b_plane, b_rows, plane, rows)


def sections_kernel(size_x, size_y, columns, planes, weight_y, weight_z, out, *refs):
    held, planes_in, y_in, z_in, sems = refs
    own = planes.shape[0]
    box_y, box_z = weight_y.shape[0], weight_z.shape[0]
    part = box_y // (columns * size_x)
    moves = [(weight_y, y_in), (weight_z, z_in)]
    moves += [(planes.at[t], planes_in.at[t]) for t in range(own)]
    copies = [pltpu.make_async_copy(*move, sems.at[k]) for k, move in enumerate(moves)]
    for copy in copies:
        copy.start()
    out[...] = jnp.zeros_like(out)
    held[...] = jnp.zeros_like(held)
    copies[0].wait()
    copies[1].wait()
    in_y, in_z = split(y_in[...]), split(z_in[...])
    for t in range(own):
        copies[2 + t].wait()
        partly = split(dot(in_y, split(planes_in[t])))
        held[t, strip : strip + box_y, :box_z] = dot(partly, in_z, ((1,), (1,)))
    for k in range(columns):
        for i in range(size_x):
            start = strip + (k * size_x + i) * part - 1
            for t in range(own):
                piece = held[t, start : start + part + 1]
                row = t * (part + 1)
                out[i * size_y + size_y - columns + k, row : row + part + 1] = piece


def sections(planes, weight_y, weight_z, size_x, size_y, columns, height):
    own, box_y = planes.shape[0], weight_y.shape[0]
    return pl.pallas_call(
        functools.partial(sections_kernel, size_x, size_y, columns),
        in_specs=[pl.BlockSpec(memory_space=pltpu.HBM)] * 3,
        out_shape=f32(size_x * size_y, height, lanes),
        scratch_shapes=[
            pltpu.VMEM((own, strip + box_y, lanes), jnp.float32),
            *[pltpu.VMEM(a.shape, jnp.float32) for a in (planes, weight_y, weight_z)],
            pltpu.SemaphoreType.DMA((2 + own,)),
        ],
        compiler_params=pltpu.CompilerParams(vmem_limit_bytes=16 << 20),
        name="sections",
    )(*map(in_hbm, (planes, weight_y, weight_z)))


def contract_kernel(own, part, nx, anchor, weight_x, gathered, out, padded):
    box_x, count = weight_x.shape
    size_x = out.shape[0]
    span = nx + 1
    devices = count // own
    stride = gathered.shape[0] // devices
    section = lax.broadcasted_iota(jnp.int32, (count, count), 0)
    column = lax.broadcasted_iota(jnp.int32, (count, count), 1)
    pick = section == own * lax.rem(column, devices) + lax.div(column, devices)
    pick = pick.astype(jnp.bfloat16)
    weights = [dot([w], [pick]).astype(jnp.bfloat16) for w in split(weight_x[...])]
    padded[...] = jnp.zeros_like(padded)
    for r in range(part + 1):
        terms = [
            gathered[pl.ds(t * (part + 1) + r, devices, stride=stride), :] for t in range(own)
        ]
        box = dot(weights, split(jnp.concatenate(terms, 0)))
        padded[r, pl.ds(anchor[0] + strip, box_x), :] = box
    for i in range(size_x):
        start = strip + i * nx
        for r in range(part + 1):
            out[i, r * span : r * span + nx] = padded[r, start : start + nx]
            out[i, r * span + nx : (r + 1) * span] = padded[r, start - 1 : start]
        left = out.shape[1] - (part + 1) * span
        out[i, (part + 1) * span :] = jnp.zeros((left, lanes), jnp.float32)


def contract(anchor, weight_x, gathered, own, part, nx, size_x):
    height = -(-(part + 1) * (nx + 1) // strip) * strip
    return pl.pallas_call(
        functools.partial(contract_kernel, own, part, nx),
        in_specs=[
            pl.BlockSpec(memory_space=pltpu.SMEM),
            pl.BlockSpec(memory_space=pltpu.VMEM),
            pl.BlockSpec(memory_space=pltpu.VMEM),
        ],
        out_shape=f32(size_x, height, lanes),
        scratch_shapes=[pltpu.VMEM((part + 1, 2 * strip + size_x * nx, lanes), jnp.float32)],
        compiler_params=pltpu.CompilerParams(vmem_limit_bytes=16 << 20),
        name="contract",
    )(anchor, weight_x, gathered)


def place_kernel(part, anchor, box, cells, rate_plane, rate_rows, *refs):
    out, out_plane, out_rows, held = refs
    size_x = box.shape[0]
    _, ny, nz = out.shape
    nx = out.shape[0] - 1
    span = nx + 1
    for i in range(size_x):
        for r in range(part):
            y = i * part + r
            first = (r + 1) * span
            held[pl.ds(y, nx, stride=ny), :] = box[i, first : first + nx]
            held[nx * ny + y : nx * ny + y + 1] = box[i, first + nx : first + nx + 1]
    cell = lax.broadcasted_iota(jnp.int32, (lanes, nz), 1)
    which = lax.broadcasted_iota(jnp.int32, (lanes, nz), 0)
    pick = (cell - anchor[2] == which).astype(jnp.bfloat16)

    def placed(values):
        return (-time_step) * dot(split(values, 3), [pick])

    def lost(values, rates):
        return jnp.exp(-time_step * rates) * placed(values)

    for t in range(0, nx, 4):
        values = placed(held[t * ny : (t + 4) * ny])
        for u in range(4):
            decay = jnp.exp(-time_step * cells[3, t + u])
            out[t + u + 1] = decay * values[u * ny : (u + 1) * ny]
    out[0] = jnp.zeros((ny, nz), jnp.float32)
    out_plane[...] = lost(held[nx * ny :], rate_plane[3])
    out_rows[...] = lost(box[0, 0:nx], rate_rows[3])


def place(anchor, box, cells, rate_plane, rate_rows, part):
    nx, ny, nz = cells.shape[1] - 1, *cells.shape[2:]
    on_chip = pl.BlockSpec(memory_space=pltpu.VMEM)
    return pl.pallas_call(
        functools.partial(place_kernel, part),
        in_specs=[pl.BlockSpec(memory_space=pltpu.SMEM)] + [on_chip] * 4,
        out_specs=(on_chip,) * 3,
        out_shape=(pltpu.VMEM((nx + 1, ny, nz), jnp.float32), f32(ny, nz), f32(nx, nz)),
        scratch_shapes=[pltpu.VMEM(((nx + 1) * ny, lanes), jnp.float32)],
        compiler_params=pltpu.CompilerParams(vmem_limit_bytes=12 << 20),
        name="place",
    )(anchor, box, in_vmem(cells), rate_plane, rate_rows)


def second_edges_kernel(*refs):
    part_plane, part_rows, b_plane, b_rows, plane, rows = refs[:6]
    source, source_plane, source_rows, first_plane, first_rows = refs[6:]
    take_halo(part_plane, part_rows, b_plane, b_rows, plane, rows, first_plane, first_rows)
    q_plane, q_rows = source_plane[...], source_rows[...]
    factor = time_step * b_plane[...]
    own = source[1]
    first_plane[0] = first_plane[0] + factor * (own - q_plane)
    first_plane[1] = first_plane[1] + factor * (own - after_row(own, q_rows[0:1]))
    first_plane[2] = first_plane[2] + factor * (own - shifted_up(own))
    factor = time_step * b_rows[...]
    own = source[1:, 0]
    first_rows[0] = first_rows[0] + factor * (own - after_row(own, q_plane[0:1]))
    first_rows[1] = first_rows[1] + factor * (own - q_rows)
    first_rows[2] = first_rows[2] + factor * (own - shifted_up(own))


def second_edges(parts, plane, rows, source):
    on_chip = pl.BlockSpec(memory_space=pltpu.VMEM)
    return pl.pallas_call(
        second_edges_kernel,
        in_specs=[on_chip] * 9,
        out_specs=(on_chip,) * 2,
        out_shape=(f32(*parts[0].shape), f32(*parts[1].shape)),
        compiler_params=pltpu.CompilerParams(vmem_limit_bytes=8 << 20),
        name="second_edges",
    )(*parts, plane, rows, in_vmem(source[0]), *source[1:])


def step_kernel(kind, *refs):
    with_source = kind != "first"
    if kind == "velocity":
        cells, source, plane, rows, source_plane, source_rows = refs[2:8]
        out_velocity, stress, velocity, out_sems = refs[8:]
    elif kind == "stress":
        cells, source, upper_plane, upper_rows = refs[2:6]
        out_stress, stress, velocity, out_sems = refs[6:]
    else:
        fields, (plane, rows, upper_plane, upper_rows) = refs[:6], refs[6:10]
        stress, velocity, cells, last_plane, last_rows, part_plane, part_rows = refs[10:17]
        in_sems = refs[17]
    nx, ny, nz = cells.shape[1] - 1, *cells.shape[2:]
    chunks = nx // per

    def arriving(k):
        here, above = pl.ds(k * per, per), pl.ds(k * per + 1, per)
        moves = [
            (fields[0].at[:, here], stress.at[:, above]),
            (fields[1].at[:, here], velocity.at[:, here]),
        ]
        for n, field in enumerate(fields[2:6]):
            moves.append((field.at[here], cells.at[n, here]))
        return [pltpu.make_async_copy(*m, in_sems.at[k, n]) for n, m in enumerate(moves)]

    def leaving(k):
        here, above = pl.ds(k * per, per), pl.ds(k * per + 1, per)
        if kind == "velocity":
            move = (velocity.at[:, here], out_velocity.at[:, here])
        else:
            move = (stress.at[:, above], out_stress.at[:, here])
        return [pltpu.make_async_copy(*move, out_sems.at[k])]

    def every(make, act):
        def one(n, _):
            for copy in make(chunks - 1 - n):
                act(copy)
            return 0

        lax.fori_loop(0, chunks, one, 0)

    if not with_source:
        every(arriving, lambda copy: copy.start())
    if kind != "stress":
        for c, which in enumerate((0, 3, 4)):
            stress[which, 0] = plane[c]
        if with_source:
            stress[0, 0] = plane[0] + source_plane[...]
    if kind != "velocity":
        for c in range(3):
            velocity[c, nx] = upper_plane[c]

    top = lax.broadcasted_iota(jnp.int32, (strip, nz), 0) == 0
    bottom = lax.broadcasted_iota(jnp.int32, (strip, nz), 0) == strip - 1

    def velocity_plane(x):
        above = [rows[c, pl.ds(x, 1)] for c in range(3)]
        if with_source:
            above[1] = above[1] + source_rows[pl.ds(x, 1)]
        above = [jnp.broadcast_to(row, (strip, nz)) for row in above]
        for r in range(ny // strip):
            here = slice(strip * r, strip * (r + 1))
            s = [stress[c, x + 1, here] for c in range(6)]
            before = [stress[c, x, here] for c in (0, 3, 4)]
            if with_source:
                extra = source[x + 1, here]
                s[:3] = [value + extra for value in s[:3]]
                before[0] = before[0] + source[x, here]
            s_xx, s_yy, s_zz, s_xy, s_xz, s_yz = s
            rolled = [pltpu.roll(value, 1, 0) for value in (s_xy, s_yy, s_yz)]
            up = [jnp.where(top, above[c], rolled[c]) for c in range(3)]
            factor = time_step * cells[0, x, here]
            sums = (
                (s_xx - before[0]) + (s_xy - up[0]) + (s_xz - shifted_up(s_xz)),
                (s_xy - before[1]) + (s_yy - up[1]) + (s_yz - shifted_up(s_yz)),
                (s_xz - before[2]) + (s_yz - up[2]) + (s_zz - shifted_up(s_zz)),
            )
            for c in range(3):
                velocity[c, x, here] = velocity[c, x, here] + factor * sums[c]
            above = rolled

    def stress_plane(x):
        below = [jnp.broadcast_to(upper_rows[c, pl.ds(x, 1)], (strip, nz)) for c in range(3)]
        for r in reversed(range(ny // strip)):
            here = slice(strip * r, strip * (r + 1))
            v = [velocity[c, x, here] for c in range(3)]
            rolled = [pltpu.roll(value, strip - 1, 0) for value in v]
            in_x = [velocity[c, x + 1, here] - v[c] for c in range(3)]
            in_y = [jnp.where(bottom, below[c], rolled[c]) - v[c] for c in range(3)]
            in_z = [shifted_down(v[c]) - v[c] for c in range(3)]
            decay = jnp.exp(-time_step * cells[3, x, here])
            shear = time_step * cells[2, x, here]
            normal = [in_x[0], in_y[1], in_z[2]]
            common = time_step * cells[1, x, here] * (normal[0] + normal[1] + normal[2])
            twice = 2.0 * shear
            if with_source:
                extra = source[x + 1, here]
                common = common + extra
            values = []
            for c in range(3):
                value = decay * (stress[c, x + 1, here] + (common + twice * normal[c]))
                values.append(value + extra if with_source else value)
            for c, (a, b) in enumerate(
                ((in_y[0], in_x[1]), (in_z[0], in_x[2]), (in_z[1], in_y[2])), 3
            ):
                values.append(decay * (stress[c, x + 1, here] + shear * (a + b)))
            for c in range(6):
                stress[c, x + 1, here] = values[c]
            if not with_source and r == ny // strip - 1:
                for c, which in enumerate((3, 1, 5)):
                    last_rows[c, pl.ds(x, 1)] = values[which][strip - 1 :]
            below = rolled

    def one_chunk(n, _):
        k = chunks - 1 - n

        if not with_source:

            @pl.when(k > 0)
            def _():
                for copy in arriving(k - 1):
                    copy.wait()

        def one_plane(m, _):
            x = k * per + (per - 1 - m)
            if kind != "stress":
                velocity_plane(x)
            if kind != "velocity":
                stress_plane(x)
            return 0

        lax.fori_loop(0, per, one_plane, 0, unroll=True)
        if with_source:
            for copy in leaving(k):
                copy.start()
        return 0

    if not with_source:
        for copy in arriving(chunks - 1):
            copy.wait()
    lax.fori_loop(0, chunks, one_chunk, 0)
    if with_source:
        every(leaving, lambda copy: copy.wait())
    else:
        for c, which in enumerate((0, 3, 4)):
            last_plane[c] = stress[which, nx]
        partial_velocity(
            [stress[c, 1] for c in range(6)],
            [velocity[c, 0] for c in range(3)],
            time_step * cells[0, 0],
            part_plane,
            (nothing, row_before),
        )
        partial_velocity(
            [stress[c, 1:, 0] for c in range(6)],
            [velocity[c, :nx, 0] for c in range(3)],
            time_step * cells[0, :nx, 0],
            part_rows,
            (row_before, nothing),
        )


def estimate(nx, ny, nz, words):
    count = nx * ny * nz
    return pl.CostEstimate(
        flops=100 * count, bytes_accessed=4 * words * count, transcendentals=count
    )


def first_step(stress, velocity, coefficients, plane, rows, upper_plane, upper_rows):
    _, nx, ny, nz = velocity.shape
    fields = [in_hbm(a) for a in (stress, velocity, *coefficients)]
    on_chip = pl.BlockSpec(memory_space=pltpu.VMEM)
    return pl.pallas_call(
        functools.partial(step_kernel, "first"),
        in_specs=[pl.BlockSpec(memory_space=pltpu.HBM)] * len(fields) + [on_chip] * 4,
        out_specs=(on_chip,) * 7,
        out_shape=(
            *[pltpu.VMEM((n, nx + 1, ny, nz), jnp.float32) for n in (6, 3, 4)],
            *[f32(3, ny, nz), f32(3, nx, nz)] * 2,
        ),
        scratch_shapes=[pltpu.SemaphoreType.DMA((nx // per, len(fields)))],
        compiler_params=pltpu.CompilerParams(vmem_limit_bytes=20 << 20),
        cost_estimate=estimate(nx, ny, nz, 13),
        name="first_step",
    )(*fields, plane, rows, upper_plane, upper_rows)


def second_step(kind, stress, velocity, cells, source, edges):
    nx, ny, nz = cells.shape[1] - 1, *cells.shape[2:]
    held = [in_vmem(a) for a in (stress, velocity, cells, source)]
    on_chip = pl.BlockSpec(memory_space=pltpu.VMEM)
    parts = 3 if kind == "velocity" else 6
    return pl.pallas_call(
        functools.partial(step_kernel, kind),
        in_specs=[on_chip] * (len(held) + len(edges)),
        out_specs=(pl.BlockSpec(memory_space=pltpu.HBM), on_chip, on_chip),
        out_shape=(
            pltpu.HBM((parts, nx, ny, nz), jnp.float32),
            *[pltpu.VMEM(a.shape, jnp.float32) for a in (stress, velocity)],
        ),
        input_output_aliases={0: 1, 1: 2},
        scratch_shapes=[pltpu.SemaphoreType.DMA((nx // per,))],
        compiler_params=pltpu.CompilerParams(vmem_limit_bytes=20 << 20),
        cost_estimate=estimate(nx, ny, nz, parts),
        name="second_" + kind,
    )(*held, *edges)


def shards(
    source_planes,
    weight_x,
    weight_y,
    weight_z,
    box_anchor,
    velocity,
    stress,
    lame_lambda,
    lame_mu,
    buoyancy,
    attenuation,
):
    nx, ny, nz = lame_mu.shape
    box_x, sources = weight_x.shape
    box_y = weight_y.shape[0]
    size_x, size_y = lax.axis_size("gx"), lax.axis_size("gy")
    own = source_planes.shape[0]
    columns = box_y // ny
    part = ny // size_x
    height = -(-own * (part + 1) // strip) * strip
    coefficients = (buoyancy, lame_lambda, lame_mu, attenuation)

    pieces = sections(source_planes, weight_y, weight_z, size_x, size_y, columns, height)
    gathered = lax.all_to_all(pieces, ("gx", "gy"), 0, 0, tiled=True)
    send_x, send_y, *parts = edges(stress, velocity, buoyancy, attenuation)
    plane = neighbour(send_x, "gx", 1)
    rows = neighbour(send_y, "gy", 1)
    first_x, first_y = first_edges(*parts, plane, rows)

    gathered, first_x, first_y = lax.optimization_barrier((gathered, first_x, first_y))
    gathered = gathered.reshape(size_x * size_y * height, lanes)
    shares = contract(box_anchor, weight_x, gathered, own, part, nx, size_x)
    shares, first_x, first_y = lax.optimization_barrier((shares, first_x, first_y))
    box = lax.all_to_all(shares, "gx", 0, 0, tiled=True)
    upper_x = neighbour(first_x, "gx", -1)
    upper_y = neighbour(first_y, "gy", -1)
    box, upper_x, upper_y = lax.optimization_barrier((box, upper_x, upper_y))

    strained, speed, cells, last_x, last_y, *parts[:2] = first_step(
        stress, velocity, coefficients, plane, rows, upper_x, upper_y
    )
    lower_x = neighbour(last_x, "gx", 1)
    lower_y = neighbour(last_y, "gy", 1)
    source = place(box_anchor, box, cells, plane, rows, part)
    first_x, first_y = second_edges(parts, lower_x, lower_y, source)
    upper_x = neighbour(first_x, "gx", -1)
    upper_y = neighbour(first_y, "gy", -1)
    velocity_out, strained, speed = second_step(
        "velocity", strained, speed, cells, source[0], (lower_x, lower_y, *source[1:])
    )
    stress_out, _, _ = second_step(
        "stress", strained, speed, cells, source[0], (upper_x, upper_y)
    )
    return (velocity_out, stress_out)


def solution(mesh):
    in_specs = (
        P(("gx", "gy"), None, None),
        P(),
        P(),
        P(),
        P(),
        P(None, "gx", "gy", None),
        P(None, "gx", "gy", None),
        P("gx", "gy", None),
        P("gx", "gy", None),
        P("gx", "gy", None),
        P("gx", "gy", None),
    )
    out_specs = (P(None, "gx", "gy", None), P(None, "gx", "gy", None))
    return jax.shard_map(shards, mesh=mesh, in_specs=in_specs, out_specs=out_specs, check_vma=False)
```

```python
import functools

import jax
import jax.numpy as jnp
from jax import lax
from jax.experimental import pallas as pl
from jax.experimental.pallas import tpu as pltpu
from jax.sharding import PartitionSpec as P

time_step = 0.2
strip = 8
lanes = 128
per = 3


def neighbour(value, axis, by):
    size = lax.axis_size(axis)
    pairs = [(i, i + by) for i in range(size) if 0 <= i + by < size]
    return lax.ppermute(value, axis, pairs)


def in_hbm(value):
    return pltpu.with_memory_space_constraint(value, pltpu.HBM)


def in_vmem(value):
    return pltpu.with_memory_space_constraint(value, pltpu.VMEM)


def f32(*shape):
    return jax.ShapeDtypeStruct(shape, jnp.float32)


def split(values, parts=2):
    out = []
    for _ in range(parts):
        out.append(values.astype(jnp.bfloat16))
        values = values - out[-1].astype(jnp.float32)
    return out


def dot(a, b, contract=((1,), (0,))):
    return sum(
        lax.dot_general(
            a[i], b[j], (contract, ((), ())), preferred_element_type=jnp.float32
        )
        for i, j in sorted(
            ((i, j) for i in range(len(a)) for j in range(len(b))), key=lambda ij: -sum(ij)
        )
        if i + j < max(len(a), len(b))
    )


def shifted_up(values):
    first = jnp.zeros((values.shape[0], 1), jnp.float32)
    return jnp.concatenate([first, values[:, :-1]], 1)


def shifted_down(values):
    last = jnp.zeros((values.shape[0], 1), jnp.float32)
    return jnp.concatenate([values[:, 1:], last], 1)


def after_row(values, row):
    where = lax.broadcasted_iota(jnp.int32, values.shape, 0)
    return jnp.where(where == 0, row, pltpu.roll(values, 1, 0))


def partial_velocity(stress, velocity, factor, out, before):
    xx, yy, zz, xy, xz, yz = stress
    along_x, along_y = before
    out[0] = velocity[0] + factor * (
        (xx - along_x(xx)) + (xy - along_y(xy)) + (xz - shifted_up(xz))
    )
    out[1] = velocity[1] + factor * (
        (xy - along_x(xy)) + (yy - along_y(yy)) + (yz - shifted_up(yz))
    )
    out[2] = velocity[2] + factor * (
        (xz - along_x(xz)) + (yz - along_y(yz)) + (zz - shifted_up(zz))
    )


def nothing(values):
    return jnp.zeros_like(values)


def row_before(values):
    return after_row(values, 0.0)


def edges_kernel(stress, velocity, buoyancy, attenuation, *refs):
    out_plane, out_rows, part_plane, part_rows, b_plane, b_rows = refs[:6]
    s_plane, s_rows, v_plane, v_rows, sems = refs[6:]
    _, nx, ny, _ = stress.shape
    moves = [
        (stress.at[:, 0], s_plane),
        (stress.at[:, :, 0], s_rows),
        (velocity.at[:, 0], v_plane),
        (velocity.at[:, :, 0], v_rows),
        (buoyancy.at[0], b_plane),
        (buoyancy.at[:, 0], b_rows),
        (stress.at[0, nx - 1], out_plane.at[0]),
        (stress.at[3:5, nx - 1], out_plane.at[1:3]),
        (attenuation.at[nx - 1], out_plane.at[3]),
        (stress.at[3, :, ny - 1], out_rows.at[0]),
        (stress.at[1, :, ny - 1], out_rows.at[1]),
        (stress.at[5, :, ny - 1], out_rows.at[2]),
        (attenuation.at[:, ny - 1], out_rows.at[3]),
    ]
    copies = [pltpu.make_async_copy(*move, sems.at[k]) for k, move in enumerate(moves)]
    for copy in copies:
        copy.start()
    for copy in copies:
        copy.wait()
    partial_velocity(
        [s_plane[c] for c in range(6)],
        [v_plane[c] for c in range(3)],
        time_step * b_plane[...],
        part_plane,
        (nothing, row_before),
    )
    partial_velocity(
        [s_rows[c] for c in range(6)],
        [v_rows[c] for c in range(3)],
        time_step * b_rows[...],
        part_rows,
        (row_before, nothing),
    )


def edges(stress, velocity, buoyancy, attenuation):
    _, nx, ny, nz = stress.shape
    return pl.pallas_call(
        edges_kernel,
        in_specs=[pl.BlockSpec(memory_space=pltpu.HBM)] * 4,
        out_shape=(
            f32(4, ny, nz),
            f32(4, nx, nz),
            f32(3, ny, nz),
            f32(3, nx, nz),
            f32(ny, nz),
            f32(nx, nz),
        ),
        scratch_shapes=[
            pltpu.VMEM((6, ny, nz), jnp.float32),
            pltpu.VMEM((6, nx, nz), jnp.float32),
            pltpu.VMEM((3, ny, nz), jnp.float32),
            pltpu.VMEM((3, nx, nz), jnp.float32),
            pltpu.SemaphoreType.DMA((13,)),
        ],
        compiler_params=pltpu.CompilerParams(vmem_limit_bytes=8 << 20),
        name="edges",
    )(*map(in_hbm, (stress, velocity, buoyancy, attenuation)))


def take_halo(part_plane, part_rows, b_plane, b_rows, plane, rows, out_plane, out_rows):
    factor_plane, factor_rows = time_step * b_plane[...], time_step * b_rows[...]
    for c in range(3):
        first_row = lax.broadcasted_iota(jnp.int32, factor_plane.shape, 0) == 0
        corner = jnp.where(first_row, rows[c, 0:1], 0.0)
        out_plane[c] = part_plane[c] - factor_plane * (plane[c] + corner)
        first_row = lax.broadcasted_iota(jnp.int32, factor_rows.shape, 0) == 0
        corner = jnp.where(first_row, plane[c, 0:1], 0.0)
        out_rows[c] = part_rows[c] - factor_rows * (rows[c] + corner)


def first_edges(part_plane, part_rows, b_plane, b_rows, plane, rows):
    return pl.pallas_call(
        take_halo,
        out_shape=(f32(*part_plane.shape), f32(*part_rows.shape)),
        compiler_params=pltpu.CompilerParams(vmem_limit_bytes=8 << 20),
        name="first_edges",
    )(part_plane, part_rows, b_plane, b_rows, plane, rows)


def sections_kernel(size_x, size_y, columns, planes, weight_y, weight_z, out, *refs):
    held, planes_in, y_in, z_in, sems = refs
    own = planes.shape[0]
    box_y, box_z = weight_y.shape[0], weight_z.shape[0]
    part = box_y // (columns * size_x)
    moves = [(weight_y, y_in), (weight_z, z_in)]
    moves += [(planes.at[t], planes_in.at[t]) for t in range(own)]
    copies = [pltpu.make_async_copy(*move, sems.at[k]) for k, move in enumerate(moves)]
    for copy in copies:
        copy.start()
    out[...] = jnp.zeros_like(out)
    held[...] = jnp.zeros_like(held)
    copies[0].wait()
    copies[1].wait()
    in_y, in_z = split(y_in[...]), split(z_in[...])
    for t in range(own):
        copies[2 + t].wait()
        partly = split(dot(in_y, split(planes_in[t])))
        held[t, strip : strip + box_y, :box_z] = dot(partly, in_z, ((1,), (1,)))
    free = lax.broadcasted_iota(jnp.int32, (1, lanes), 1) >= box_z
    width = lanes - box_z
    for k in range(columns):
        for i in range(size_x):
            start = strip + (k * size_x + i) * part
            device = i * size_y + size_y - columns + k
            for t in range(own):
                row = (device * own + t) * part
                out[row : row + part] = held[t, start : start + part]
                for p in range(box_z // width if i == 0 and k > 0 else 0):
                    ahead = pltpu.roll(held[t, start - 1 : start], box_z - p * width, 1)
                    here = held[t, start + p : start + p + 1]
                    out[row + p : row + p + 1] = jnp.where(free, ahead, here)


def sections(planes, weight_y, weight_z, size_x, size_y, columns):
    own, box_y = planes.shape[0], weight_y.shape[0]
    height = own * (box_y // (columns * size_x))
    return pl.pallas_call(
        functools.partial(sections_kernel, size_x, size_y, columns),
        in_specs=[pl.BlockSpec(memory_space=pltpu.HBM)] * 3,
        out_shape=f32(size_x * size_y * height, lanes),
        scratch_shapes=[
            pltpu.VMEM((own, strip + box_y, lanes), jnp.float32),
            *[pltpu.VMEM(a.shape, jnp.float32) for a in (planes, weight_y, weight_z)],
            pltpu.SemaphoreType.DMA((2 + own,)),
        ],
        compiler_params=pltpu.CompilerParams(vmem_limit_bytes=16 << 20),
        name="sections",
    )(*map(in_hbm, (planes, weight_y, weight_z)))


def contract_kernel(own, part, nx, anchor, weight_x, gathered, out, padded):
    box_x, count = weight_x.shape
    size_x = out.shape[0]
    span = nx + 1
    devices = count // own
    stride = own * part
    section = lax.broadcasted_iota(jnp.int32, (count, count), 0)
    column = lax.broadcasted_iota(jnp.int32, (count, count), 1)
    pick = section == own * lax.rem(column, devices) + lax.div(column, devices)
    pick = pick.astype(jnp.bfloat16)
    weights = [dot([w], [pick]).astype(jnp.bfloat16) for w in split(weight_x[...])]
    padded[...] = jnp.zeros_like(padded)
    for r in range(part):
        terms = [gathered[pl.ds(t * part + r, devices, stride=stride), :] for t in range(own)]
        box = dot(weights, split(jnp.concatenate(terms, 0)))
        padded[r, pl.ds(anchor[0] + strip, box_x), :] = box
    for i in range(size_x):
        start = strip + i * nx
        for r in range(part):
            out[i, r * span : r * span + nx] = padded[r, start : start + nx]
            out[i, r * span + nx : (r + 1) * span] = padded[r, start - 1 : start]
        left = out.shape[1] - part * span
        out[i, part * span :] = jnp.zeros((left, lanes), jnp.float32)


def contract(anchor, weight_x, gathered, own, part, nx, size_x):
    height = -(-part * (nx + 1) // strip) * strip
    return pl.pallas_call(
        functools.partial(contract_kernel, own, part, nx),
        in_specs=[
            pl.BlockSpec(memory_space=pltpu.SMEM),
            pl.BlockSpec(memory_space=pltpu.VMEM),
            pl.BlockSpec(memory_space=pltpu.VMEM),
        ],
        out_shape=f32(size_x, height, lanes),
        scratch_shapes=[pltpu.VMEM((part, 2 * strip + size_x * nx, lanes), jnp.float32)],
        compiler_params=pltpu.CompilerParams(vmem_limit_bytes=16 << 20),
        name="contract",
    )(anchor, weight_x, gathered)


def place_kernel(part, box_z, anchor, box, cells, rate_plane, rate_rows, *refs):
    out, out_plane, out_rows, held = refs
    size_x = box.shape[0]
    _, ny, nz = out.shape
    nx = out.shape[0] - 1
    span = nx + 1
    for i in range(size_x):
        for r in range(part):
            y = i * part + r
            first = r * span
            held[pl.ds(y, nx, stride=ny), :] = box[i, first : first + nx]
            held[nx * ny + y : nx * ny + y + 1] = box[i, first + nx : first + nx + 1]
    cell = lax.broadcasted_iota(jnp.int32, (lanes, nz), 1)
    which = lax.broadcasted_iota(jnp.int32, (lanes, nz), 0)
    pick = ((cell - anchor[2] == which) & (which < box_z)).astype(jnp.bfloat16)

    def placed(values):
        return (-time_step) * dot(split(values, 3), [pick])

    def lost(values, rates):
        return jnp.exp(-time_step * rates) * placed(values)

    for t in range(0, nx, 4):
        values = placed(held[t * ny : (t + 4) * ny])
        for u in range(4):
            decay = jnp.exp(-time_step * cells[3, t + u])
            out[t + u + 1] = decay * values[u * ny : (u + 1) * ny]
    out[0] = jnp.zeros((ny, nz), jnp.float32)
    out_plane[...] = lost(held[nx * ny :], rate_plane[3])
    width = lanes - box_z
    piece = lax.div(lax.broadcasted_iota(jnp.int32, (nx, lanes), 1), width)
    ahead = jnp.zeros((nx, lanes), jnp.float32)
    for p in range(box_z // width):
        values = pltpu.roll(box[0, p * span : p * span + nx], lanes - box_z + p * width, 1)
        ahead = jnp.where(piece == p, values, ahead)
    out_rows[...] = lost(ahead, rate_rows[3])


def place(anchor, box, cells, rate_plane, rate_rows, part, box_z):
    nx, ny, nz = cells.shape[1] - 1, *cells.shape[2:]
    on_chip = pl.BlockSpec(memory_space=pltpu.VMEM)
    return pl.pallas_call(
        functools.partial(place_kernel, part, box_z),
        in_specs=[pl.BlockSpec(memory_space=pltpu.SMEM)] + [on_chip] * 4,
        out_specs=(on_chip,) * 3,
        out_shape=(pltpu.VMEM((nx + 1, ny, nz), jnp.float32), f32(ny, nz), f32(nx, nz)),
        scratch_shapes=[pltpu.VMEM(((nx + 1) * ny, lanes), jnp.float32)],
        compiler_params=pltpu.CompilerParams(vmem_limit_bytes=12 << 20),
        name="place",
    )(anchor, box, in_vmem(cells), rate_plane, rate_rows)


def second_edges_kernel(*refs):
    part_plane, part_rows, b_plane, b_rows, plane, rows = refs[:6]
    source, source_plane, source_rows, first_plane, first_rows = refs[6:]
    take_halo(part_plane, part_rows, b_plane, b_rows, plane, rows, first_plane, first_rows)
    q_plane, q_rows = source_plane[...], source_rows[...]
    factor = time_step * b_plane[...]
    own = source[1]
    first_plane[0] = first_plane[0] + factor * (own - q_plane)
    first_plane[1] = first_plane[1] + factor * (own - after_row(own, q_rows[0:1]))
    first_plane[2] = first_plane[2] + factor * (own - shifted_up(own))
    factor = time_step * b_rows[...]
    own = source[1:, 0]
    first_rows[0] = first_rows[0] + factor * (own - after_row(own, q_plane[0:1]))
    first_rows[1] = first_rows[1] + factor * (own - q_rows)
    first_rows[2] = first_rows[2] + factor * (own - shifted_up(own))


def second_edges(parts, plane, rows, source):
    on_chip = pl.BlockSpec(memory_space=pltpu.VMEM)
    return pl.pallas_call(
        second_edges_kernel,
        in_specs=[on_chip] * 9,
        out_specs=(on_chip,) * 2,
        out_shape=(f32(*parts[0].shape), f32(*parts[1].shape)),
        compiler_params=pltpu.CompilerParams(vmem_limit_bytes=8 << 20),
        name="second_edges",
    )(*parts, plane, rows, in_vmem(source[0]), *source[1:])


def step_kernel(kind, *refs):
    with_source = kind != "first"
    if kind == "velocity":
        cells, source, plane, rows, source_plane, source_rows = refs[2:8]
        out_velocity, stress, velocity, out_sems = refs[8:]
    elif kind == "stress":
        cells, source, upper_plane, upper_rows = refs[2:6]
        out_stress, stress, velocity, out_sems = refs[6:]
    else:
        fields, (plane, rows, upper_plane, upper_rows) = refs[:6], refs[6:10]
        stress, velocity, cells, last_plane, last_rows, part_plane, part_rows = refs[10:17]
        in_sems = refs[17]
    nx, ny, nz = cells.shape[1] - 1, *cells.shape[2:]
    chunks = nx // per

    def arriving(k):
        here, above = pl.ds(k * per, per), pl.ds(k * per + 1, per)
        moves = [
            (fields[0].at[:, here], stress.at[:, above]),
            (fields[1].at[:, here], velocity.at[:, here]),
        ]
        for n, field in enumerate(fields[2:6]):
            moves.append((field.at[here], cells.at[n, here]))
        return [pltpu.make_async_copy(*m, in_sems.at[k, n]) for n, m in enumerate(moves)]

    def leaving(k):
        here, above = pl.ds(k * per, per), pl.ds(k * per + 1, per)
        if kind == "velocity":
            move = (velocity.at[:, here], out_velocity.at[:, here])
        else:
            move = (stress.at[:, above], out_stress.at[:, here])
        return [pltpu.make_async_copy(*move, out_sems.at[k])]

    def every(make, act):
        def one(n, _):
            for copy in make(chunks - 1 - n):
                act(copy)
            return 0

        lax.fori_loop(0, chunks, one, 0)

    if not with_source:
        every(arriving, lambda copy: copy.start())
    if kind != "stress":
        for c, which in enumerate((0, 3, 4)):
            stress[which, 0] = plane[c]
        if with_source:
            stress[0, 0] = plane[0] + source_plane[...]
    if kind != "velocity":
        for c in range(3):
            velocity[c, nx] = upper_plane[c]

    top = lax.broadcasted_iota(jnp.int32, (strip, nz), 0) == 0
    bottom = lax.broadcasted_iota(jnp.int32, (strip, nz), 0) == strip - 1

    def velocity_plane(x):
        above = [rows[c, pl.ds(x, 1)] for c in range(3)]
        if with_source:
            above[1] = above[1] + source_rows[pl.ds(x, 1)]
        above = [jnp.broadcast_to(row, (strip, nz)) for row in above]
        for r in range(ny // strip):
            here = slice(strip * r, strip * (r + 1))
            s = [stress[c, x + 1, here] for c in range(6)]
            before = [stress[c, x, here] for c in (0, 3, 4)]
            if with_source:
                extra = source[x + 1, here]
                s[:3] = [value + extra for value in s[:3]]
                before[0] = before[0] + source[x, here]
            s_xx, s_yy, s_zz, s_xy, s_xz, s_yz = s
            rolled = [pltpu.roll(value, 1, 0) for value in (s_xy, s_yy, s_yz)]
            up = [jnp.where(top, above[c], rolled[c]) for c in range(3)]
            factor = time_step * cells[0, x, here]
            sums = (
                (s_xx - before[0]) + (s_xy - up[0]) + (s_xz - shifted_up(s_xz)),
                (s_xy - before[1]) + (s_yy - up[1]) + (s_yz - shifted_up(s_yz)),
                (s_xz - before[2]) + (s_yz - up[2]) + (s_zz - shifted_up(s_zz)),
            )
            for c in range(3):
                velocity[c, x, here] = velocity[c, x, here] + factor * sums[c]
            above = rolled

    def stress_plane(x):
        below = [jnp.broadcast_to(upper_rows[c, pl.ds(x, 1)], (strip, nz)) for c in range(3)]
        for r in reversed(range(ny // strip)):
            here = slice(strip * r, strip * (r + 1))
            v = [velocity[c, x, here] for c in range(3)]
            rolled = [pltpu.roll(value, strip - 1, 0) for value in v]
            in_x = [velocity[c, x + 1, here] - v[c] for c in range(3)]
            in_y = [jnp.where(bottom, below[c], rolled[c]) - v[c] for c in range(3)]
            in_z = [shifted_down(v[c]) - v[c] for c in range(3)]
            decay = jnp.exp(-time_step * cells[3, x, here])
            shear = time_step * cells[2, x, here]
            normal = [in_x[0], in_y[1], in_z[2]]
            common = time_step * cells[1, x, here] * (normal[0] + normal[1] + normal[2])
            twice = 2.0 * shear
            if with_source:
                extra = source[x + 1, here]
                common = common + extra
            values = []
            for c in range(3):
                value = decay * (stress[c, x + 1, here] + (common + twice * normal[c]))
                values.append(value + extra if with_source else value)
            for c, (a, b) in enumerate(
                ((in_y[0], in_x[1]), (in_z[0], in_x[2]), (in_z[1], in_y[2])), 3
            ):
                values.append(decay * (stress[c, x + 1, here] + shear * (a + b)))
            for c in range(6):
                stress[c, x + 1, here] = values[c]
            if not with_source and r == ny // strip - 1:
                for c, which in enumerate((3, 1, 5)):
                    last_rows[c, pl.ds(x, 1)] = values[which][strip - 1 :]
            below = rolled

    def one_chunk(n, _):
        k = chunks - 1 - n

        if not with_source:

            @pl.when(k > 0)
            def _():
                for copy in arriving(k - 1):
                    copy.wait()

        def one_plane(m, _):
            x = k * per + (per - 1 - m)
            if kind != "stress":
                velocity_plane(x)
            if kind != "velocity":
                stress_plane(x)
            return 0

        lax.fori_loop(0, per, one_plane, 0, unroll=True)
        if with_source:
            for copy in leaving(k):
                copy.start()
        return 0

    if not with_source:
        for copy in arriving(chunks - 1):
            copy.wait()
    lax.fori_loop(0, chunks, one_chunk, 0)
    if with_source:
        every(leaving, lambda copy: copy.wait())
    else:
        for c, which in enumerate((0, 3, 4)):
            last_plane[c] = stress[which, nx]
        partial_velocity(
            [stress[c, 1] for c in range(6)],
            [velocity[c, 0] for c in range(3)],
            time_step * cells[0, 0],
            part_plane,
            (nothing, row_before),
        )
        partial_velocity(
            [stress[c, 1:, 0] for c in range(6)],
            [velocity[c, :nx, 0] for c in range(3)],
            time_step * cells[0, :nx, 0],
            part_rows,
            (row_before, nothing),
        )


def estimate(nx, ny, nz, words):
    count = nx * ny * nz
    return pl.CostEstimate(
        flops=100 * count, bytes_accessed=4 * words * count, transcendentals=count
    )


def first_step(stress, velocity, coefficients, plane, rows, upper_plane, upper_rows):
    _, nx, ny, nz = velocity.shape
    fields = [in_hbm(a) for a in (stress, velocity, *coefficients)]
    on_chip = pl.BlockSpec(memory_space=pltpu.VMEM)
    return pl.pallas_call(
        functools.partial(step_kernel, "first"),
        in_specs=[pl.BlockSpec(memory_space=pltpu.HBM)] * len(fields) + [on_chip] * 4,
        out_specs=(on_chip,) * 7,
        out_shape=(
            *[pltpu.VMEM((n, nx + 1, ny, nz), jnp.float32) for n in (6, 3, 4)],
            *[f32(3, ny, nz), f32(3, nx, nz)] * 2,
        ),
        scratch_shapes=[pltpu.SemaphoreType.DMA((nx // per, len(fields)))],
        compiler_params=pltpu.CompilerParams(vmem_limit_bytes=20 << 20),
        cost_estimate=estimate(nx, ny, nz, 13),
        name="first_step",
    )(*fields, plane, rows, upper_plane, upper_rows)


def second_step(kind, stress, velocity, cells, source, edges):
    nx, ny, nz = cells.shape[1] - 1, *cells.shape[2:]
    held = [in_vmem(a) for a in (stress, velocity, cells, source)]
    on_chip = pl.BlockSpec(memory_space=pltpu.VMEM)
    parts = 3 if kind == "velocity" else 6
    return pl.pallas_call(
        functools.partial(step_kernel, kind),
        in_specs=[on_chip] * (len(held) + len(edges)),
        out_specs=(pl.BlockSpec(memory_space=pltpu.HBM), on_chip, on_chip),
        out_shape=(
            pltpu.HBM((parts, nx, ny, nz), jnp.float32),
            *[pltpu.VMEM(a.shape, jnp.float32) for a in (stress, velocity)],
        ),
        input_output_aliases={0: 1, 1: 2},
        scratch_shapes=[pltpu.SemaphoreType.DMA((nx // per,))],
        compiler_params=pltpu.CompilerParams(vmem_limit_bytes=20 << 20),
        cost_estimate=estimate(nx, ny, nz, parts),
        name="second_" + kind,
    )(*held, *edges)


def shards(
    source_planes,
    weight_x,
    weight_y,
    weight_z,
    box_anchor,
    velocity,
    stress,
    lame_lambda,
    lame_mu,
    buoyancy,
    attenuation,
):
    nx, ny, nz = lame_mu.shape
    box_x, sources = weight_x.shape
    box_y = weight_y.shape[0]
    size_x, size_y = lax.axis_size("gx"), lax.axis_size("gy")
    own = source_planes.shape[0]
    columns = box_y // ny
    part = ny // size_x
    coefficients = (buoyancy, lame_lambda, lame_mu, attenuation)

    pieces = sections(source_planes, weight_y, weight_z, size_x, size_y, columns)
    pieces = pieces.reshape(sources, part, lanes)
    gathered = lax.all_to_all(pieces, ("gx", "gy"), 0, 0, tiled=True)
    send_x, send_y, *parts = edges(stress, velocity, buoyancy, attenuation)
    plane = neighbour(send_x, "gx", 1)
    rows = neighbour(send_y, "gy", 1)
    first_x, first_y = first_edges(*parts, plane, rows)

    gathered, first_x, first_y = lax.optimization_barrier((gathered, first_x, first_y))
    gathered = gathered.reshape(sources * part, lanes)
    shares = contract(box_anchor, weight_x, gathered, own, part, nx, size_x)
    shares, first_x, first_y = lax.optimization_barrier((shares, first_x, first_y))
    box = lax.all_to_all(shares, "gx", 0, 0, tiled=True)
    upper_x = neighbour(first_x, "gx", -1)
    upper_y = neighbour(first_y, "gy", -1)
    box, upper_x, upper_y = lax.optimization_barrier((box, upper_x, upper_y))

    strained, speed, cells, last_x, last_y, *parts[:2] = first_step(
        stress, velocity, coefficients, plane, rows, upper_x, upper_y
    )
    lower_x = neighbour(last_x, "gx", 1)
    lower_y = neighbour(last_y, "gy", 1)
    source = place(box_anchor, box, cells, plane, rows, part, weight_z.shape[0])
    first_x, first_y = second_edges(parts, lower_x, lower_y, source)
    upper_x = neighbour(first_x, "gx", -1)
    upper_y = neighbour(first_y, "gy", -1)
    velocity_out, strained, speed = second_step(
        "velocity", strained, speed, cells, source[0], (lower_x, lower_y, *source[1:])
    )
    stress_out, _, _ = second_step(
        "stress", strained, speed, cells, source[0], (upper_x, upper_y)
    )
    return (velocity_out, stress_out)


def solution(mesh):
    in_specs = (
        P(("gx", "gy"), None, None),
        P(),
        P(),
        P(),
        P(),
        P(None, "gx", "gy", None),
        P(None, "gx", "gy", None),
        P("gx", "gy", None),
        P("gx", "gy", None),
        P("gx", "gy", None),
        P("gx", "gy", None),
    )
    out_specs = (P(None, "gx", "gy", None), P(None, "gx", "gy", None))
    return jax.shard_map(shards, mesh=mesh, in_specs=in_specs, out_specs=out_specs, check_vma=False)
```

```python
import functools

import jax
import jax.numpy as jnp
from jax import lax
from jax.experimental import pallas as pl
from jax.experimental.pallas import tpu as pltpu
from jax.sharding import PartitionSpec as P

time_step = 0.2
strip = 8
lanes = 128
per = 2


def neighbour(value, axis, by):
    size = lax.axis_size(axis)
    pairs = [(i, i + by) for i in range(size) if 0 <= i + by < size]
    return lax.ppermute(value, axis, pairs)


def in_hbm(value):
    return pltpu.with_memory_space_constraint(value, pltpu.HBM)


def in_vmem(value):
    return pltpu.with_memory_space_constraint(value, pltpu.VMEM)


def f32(*shape):
    return jax.ShapeDtypeStruct(shape, jnp.float32)


def split(values, parts=2):
    out = []
    for _ in range(parts):
        out.append(values.astype(jnp.bfloat16))
        values = values - out[-1].astype(jnp.float32)
    return out


def dot(a, b, contract=((1,), (0,))):
    return sum(
        lax.dot_general(
            a[i], b[j], (contract, ((), ())), preferred_element_type=jnp.float32
        )
        for i, j in sorted(
            ((i, j) for i in range(len(a)) for j in range(len(b))), key=lambda ij: -sum(ij)
        )
        if i + j < max(len(a), len(b))
    )


def shifted_up(values):
    first = jnp.zeros((values.shape[0], 1), jnp.float32)
    return jnp.concatenate([first, values[:, :-1]], 1)


def shifted_down(values):
    last = jnp.zeros((values.shape[0], 1), jnp.float32)
    return jnp.concatenate([values[:, 1:], last], 1)


def after_row(values, row):
    where = lax.broadcasted_iota(jnp.int32, values.shape, 0)
    return jnp.where(where == 0, row, pltpu.roll(values, 1, 0))


def partial_velocity(stress, velocity, factor, out, before):
    xx, yy, zz, xy, xz, yz = stress
    along_x, along_y = before
    out[0] = velocity[0] + factor * (
        (xx - along_x(xx)) + (xy - along_y(xy)) + (xz - shifted_up(xz))
    )
    out[1] = velocity[1] + factor * (
        (xy - along_x(xy)) + (yy - along_y(yy)) + (yz - shifted_up(yz))
    )
    out[2] = velocity[2] + factor * (
        (xz - along_x(xz)) + (yz - along_y(yz)) + (zz - shifted_up(zz))
    )


def nothing(values):
    return jnp.zeros_like(values)


def row_before(values):
    return after_row(values, 0.0)


def edges_kernel(between, stress, velocity, buoyancy, *refs):
    out_plane, out_rows, part_plane, part_rows, b_plane, b_rows = refs[:6]
    s_plane, s_rows, v_plane, v_rows, sems = refs[6:]
    _, nx, ny, _ = stress.shape
    moves = [
        (stress.at[:, 0], s_plane),
        (stress.at[:, :, 0], s_rows),
        (velocity.at[:, 0], v_plane),
        (velocity.at[:, :, 0], v_rows),
        (buoyancy.at[0], b_plane),
        (buoyancy.at[:, 0], b_rows),
        (stress.at[0, nx - 1], out_plane.at[0]),
        (stress.at[3:5, nx - 1], out_plane.at[1:3]),
        (stress.at[3, :, ny - 1], out_rows.at[0]),
        (stress.at[1, :, ny - 1], out_rows.at[1]),
        (stress.at[5, :, ny - 1], out_rows.at[2]),
    ]
    copies = [pltpu.make_async_copy(*move, sems.at[k]) for k, move in enumerate(moves)]
    for copy in copies:
        copy.start()
    between()
    for copy in copies:
        copy.wait()
    partial_velocity(
        [s_plane[c] for c in range(6)],
        [v_plane[c] for c in range(3)],
        time_step * b_plane[...],
        part_plane,
        (nothing, row_before),
    )
    partial_velocity(
        [s_rows[c] for c in range(6)],
        [v_rows[c] for c in range(3)],
        time_step * b_rows[...],
        part_rows,
        (row_before, nothing),
    )


def take_halo(part_plane, part_rows, b_plane, b_rows, plane, rows, out_plane, out_rows):
    factor_plane, factor_rows = time_step * b_plane[...], time_step * b_rows[...]
    for c in range(3):
        first_row = lax.broadcasted_iota(jnp.int32, factor_plane.shape, 0) == 0
        corner = jnp.where(first_row, rows[c, 0:1], 0.0)
        out_plane[c] = part_plane[c] - factor_plane * (plane[c] + corner)
        first_row = lax.broadcasted_iota(jnp.int32, factor_rows.shape, 0) == 0
        corner = jnp.where(first_row, plane[c, 0:1], 0.0)
        out_rows[c] = part_rows[c] - factor_rows * (rows[c] + corner)


def sections_kernel(size_x, size_y, columns, *refs):
    planes, weight_y, weight_z = refs[:3]
    out, (held, planes_in, y_in, z_in, sems) = refs[6], refs[13:18]
    own = planes.shape[0]
    box_y, box_z = weight_y.shape[0], weight_z.shape[0]
    part = box_y // (columns * size_x)
    moves = [(weight_y, y_in), (weight_z, z_in)]
    moves += [(planes.at[t], planes_in.at[t]) for t in range(own)]
    copies = [pltpu.make_async_copy(*move, sems.at[k]) for k, move in enumerate(moves)]
    for copy in copies:
        copy.start()

    def products():
        out[...] = jnp.zeros_like(out)
        held[...] = jnp.zeros_like(held)
        copies[0].wait()
        copies[1].wait()
        in_y, in_z = split(y_in[...]), split(z_in[...])
        for t in range(own):
            copies[2 + t].wait()
            partly = split(dot(in_y, split(planes_in[t])))
            held[t, strip : strip + box_y, :box_z] = dot(partly, in_z, ((1,), (1,)))
        free = lax.broadcasted_iota(jnp.int32, (1, lanes), 1) >= box_z
        width = lanes - box_z
        for k in range(columns):
            for i in range(size_x):
                start = strip + (k * size_x + i) * part
                device = i * size_y + size_y - columns + k
                for t in range(own):
                    row = (device * own + t) * part
                    out[row : row + part] = held[t, start : start + part]
                    for p in range(box_z // width if i == 0 and k > 0 else 0):
                        ahead = pltpu.roll(held[t, start - 1 : start], box_z - p * width, 1)
                        here = held[t, start + p : start + p + 1]
                        out[row + p : row + p + 1] = jnp.where(free, ahead, here)

    edges_kernel(products, *refs[3:6], *refs[7:13], *refs[18:])


def sections(planes, weight_y, weight_z, fields, size_x, size_y, columns):
    own, box_y = planes.shape[0], weight_y.shape[0]
    height = own * (box_y // (columns * size_x))
    nx, ny, nz = fields[2].shape
    on_chip = lambda *shape: pltpu.VMEM(shape, jnp.float32)
    return pl.pallas_call(
        functools.partial(sections_kernel, size_x, size_y, columns),
        in_specs=[pl.BlockSpec(memory_space=pltpu.HBM)] * 6,
        out_shape=(
            f32(size_x * size_y * height, lanes),
            f32(3, ny, nz),
            f32(3, nx, nz),
            f32(3, ny, nz),
            f32(3, nx, nz),
            f32(ny, nz),
            f32(nx, nz),
        ),
        scratch_shapes=[
            on_chip(own, strip + box_y, lanes),
            *[on_chip(*a.shape) for a in (planes, weight_y, weight_z)],
            pltpu.SemaphoreType.DMA((2 + own,)),
            on_chip(6, ny, nz),
            on_chip(6, nx, nz),
            on_chip(3, ny, nz),
            on_chip(3, nx, nz),
            pltpu.SemaphoreType.DMA((11,)),
        ],
        compiler_params=pltpu.CompilerParams(vmem_limit_bytes=16 << 20),
        name="sections",
    )(*map(in_hbm, (planes, weight_y, weight_z, *fields)))


def contract_kernel(own, part, nx, anchor, weight_x, gathered, *refs):
    out, padded = refs[6], refs[9]
    take_halo(*refs[:6], *refs[7:9])
    box_x, count = weight_x.shape
    size_x = out.shape[0]
    span = nx + 1
    devices = count // own
    stride = own * part
    section = lax.broadcasted_iota(jnp.int32, (count, count), 0)
    column = lax.broadcasted_iota(jnp.int32, (count, count), 1)
    pick = section == own * lax.rem(column, devices) + lax.div(column, devices)
    pick = pick.astype(jnp.bfloat16)
    weights = [dot([w], [pick]).astype(jnp.bfloat16) for w in split(weight_x[...])]
    padded[...] = jnp.zeros_like(padded)
    for r in range(part):
        terms = [gathered[pl.ds(t * part + r, devices, stride=stride), :] for t in range(own)]
        box = dot(weights, split(jnp.concatenate(terms, 0)))
        padded[r, pl.ds(anchor[0] + strip, box_x), :] = box
    for i in range(size_x):
        start = strip + i * nx
        for r in range(part):
            out[i, r * span : r * span + nx] = padded[r, start : start + nx]
            out[i, r * span + nx : (r + 1) * span] = padded[r, start - 1 : start]
        left = out.shape[1] - part * span
        out[i, part * span :] = jnp.zeros((left, lanes), jnp.float32)


def contract(anchor, weight_x, gathered, edges, own, part, nx, size_x):
    height = -(-part * (nx + 1) // strip) * strip
    return pl.pallas_call(
        functools.partial(contract_kernel, own, part, nx),
        in_specs=[pl.BlockSpec(memory_space=pltpu.SMEM)]
        + [pl.BlockSpec(memory_space=pltpu.VMEM)] * (2 + len(edges)),
        out_shape=(
            f32(size_x, height, lanes),
            f32(*edges[0].shape),
            f32(*edges[1].shape),
        ),
        scratch_shapes=[pltpu.VMEM((part, 2 * strip + size_x * nx, lanes), jnp.float32)],
        compiler_params=pltpu.CompilerParams(vmem_limit_bytes=16 << 20),
        name="contract",
    )(anchor, weight_x, gathered, *edges)


def place_kernel(part, box_z, anchor, box, cells, *refs):
    out, out_plane, out_rows, held = refs
    size_x = box.shape[0]
    _, ny, nz = out.shape
    nx = out.shape[0] - 1
    span = nx + 1
    for i in range(size_x):
        for r in range(part):
            y = i * part + r
            first = r * span
            held[pl.ds(y, nx, stride=ny), :] = box[i, first : first + nx]
            held[nx * ny + y : nx * ny + y + 1] = box[i, first + nx : first + nx + 1]
    cell = lax.broadcasted_iota(jnp.int32, (lanes, nz), 1)
    which = lax.broadcasted_iota(jnp.int32, (lanes, nz), 0)
    pick = ((cell - anchor[2] == which) & (which < box_z)).astype(jnp.bfloat16)

    def placed(values):
        return (-time_step) * dot(split(values, 3), [pick])

    for t in range(0, nx, 4):
        values = placed(held[t * ny : (t + 4) * ny])
        for u in range(4):
            decay = jnp.exp(-time_step * cells[3, t + u])
            out[t + u + 1] = decay * values[u * ny : (u + 1) * ny]
    out[0] = jnp.zeros((ny, nz), jnp.float32)
    out_plane[...] = placed(held[nx * ny :])
    width = lanes - box_z
    piece = lax.div(lax.broadcasted_iota(jnp.int32, (nx, lanes), 1), width)
    ahead = jnp.zeros((nx, lanes), jnp.float32)
    for p in range(box_z // width):
        values = pltpu.roll(box[0, p * span : p * span + nx], lanes - box_z + p * width, 1)
        ahead = jnp.where(piece == p, values, ahead)
    out_rows[...] = placed(ahead)


def place(anchor, box, cells, part, box_z):
    nx, ny, nz = cells.shape[1] - 1, *cells.shape[2:]
    on_chip = pl.BlockSpec(memory_space=pltpu.VMEM)
    return pl.pallas_call(
        functools.partial(place_kernel, part, box_z),
        in_specs=[pl.BlockSpec(memory_space=pltpu.SMEM)] + [on_chip] * 2,
        out_specs=(on_chip,) * 3,
        out_shape=(pltpu.VMEM((nx + 1, ny, nz), jnp.float32), f32(ny, nz), f32(nx, nz)),
        scratch_shapes=[pltpu.VMEM(((nx + 1) * ny, lanes), jnp.float32)],
        compiler_params=pltpu.CompilerParams(vmem_limit_bytes=12 << 20),
        name="place",
    )(anchor, box, in_vmem(cells))


def second_edges_kernel(*refs):
    part_plane, part_rows, b_plane, b_rows, plane, rows = refs[:6]
    source, box_plane, box_rows, first_plane, first_rows = refs[6:]
    take_halo(part_plane, part_rows, b_plane, b_rows, plane, rows, first_plane, first_rows)
    q_plane = jnp.exp(-time_step * plane[3]) * box_plane[...]
    q_rows = jnp.exp(-time_step * rows[3]) * box_rows[...]
    factor = time_step * b_plane[...]
    own = source[1]
    first_plane[0] = first_plane[0] + factor * (own - q_plane)
    first_plane[1] = first_plane[1] + factor * (own - after_row(own, q_rows[0:1]))
    first_plane[2] = first_plane[2] + factor * (own - shifted_up(own))
    factor = time_step * b_rows[...]
    own = source[1:, 0]
    first_rows[0] = first_rows[0] + factor * (own - after_row(own, q_plane[0:1]))
    first_rows[1] = first_rows[1] + factor * (own - q_rows)
    first_rows[2] = first_rows[2] + factor * (own - shifted_up(own))


def second_edges(parts, plane, rows, source):
    on_chip = pl.BlockSpec(memory_space=pltpu.VMEM)
    return pl.pallas_call(
        second_edges_kernel,
        in_specs=[on_chip] * 9,
        out_specs=(on_chip,) * 2,
        out_shape=tuple(f32(*a.shape) for a in parts[:2]),
        compiler_params=pltpu.CompilerParams(vmem_limit_bytes=8 << 20),
        name="second_edges",
    )(*parts, plane, rows, in_vmem(source[0]), *source[1:])


def step_kernel(kind, *refs):
    with_source = kind != "first"
    if kind == "velocity":
        stress, cells, source, velocity = refs[0], refs[2], refs[3], refs[4]
    elif kind == "inner":
        cells, source, first_plane, first_rows = refs[2:6]
        out_stress, stress, velocity, out_velocity, out_sems = refs[6:]
    elif kind == "outer":
        cells, source, upper_plane, upper_rows = refs[2:6]
        out_stress, stress, velocity, out_sems = refs[7:]
    else:
        fields, (plane, rows, upper_plane, upper_rows) = refs[:6], refs[6:10]
        stress, velocity, cells, last_plane, last_rows, part_plane, part_rows = refs[10:17]
        in_sems = refs[17]
    nx, ny, nz = cells.shape[1] - 1, *cells.shape[2:]
    chunks = nx // per

    def arriving(k):
        here, above = pl.ds(k * per, per), pl.ds(k * per + 1, per)
        moves = [
            (fields[0].at[:, here], stress.at[:, above]),
            (fields[1].at[:, here], velocity.at[:, here]),
        ]
        for n, field in enumerate(fields[2:6]):
            moves.append((field.at[here], cells.at[n, here]))
        return [pltpu.make_async_copy(*m, in_sems.at[k, n]) for n, m in enumerate(moves)]

    inner = ny - strip

    def leaving(k, first=0, count=per):
        across = slice(0, inner) if kind == "inner" else slice(inner, ny)
        here = pl.ds(k * per + first, count)
        above = pl.ds(k * per + first + 1, count)
        move = (stress.at[:, above, across], out_stress.at[:, here, across])
        return [pltpu.make_async_copy(*move, out_sems.at[k])]

    def every(make, act):
        def one(n, _):
            for copy in make(chunks - 1 - n):
                act(copy)
            return 0

        lax.fori_loop(0, chunks, one, 0)

    if not with_source:
        every(arriving, lambda copy: copy.start())
    if kind == "first":
        for c, which in enumerate((0, 3, 4)):
            stress[which, 0] = plane[c]
    if kind in ("first", "outer"):
        for c in range(3):
            velocity[c, nx] = upper_plane[c]
    if kind == "inner":
        for c in range(3):
            velocity[c, 0] = first_plane[c]
            velocity[c, :nx, 0] = first_rows[c]

    top = lax.broadcasted_iota(jnp.int32, (strip, nz), 0) == 0
    bottom = lax.broadcasted_iota(jnp.int32, (strip, nz), 0) == strip - 1

    def velocity_plane(x):
        above = [jnp.zeros((strip, nz), jnp.float32)] * 3
        if not with_source:
            above = [jnp.broadcast_to(rows[c, pl.ds(x, 1)], (strip, nz)) for c in range(3)]
        for r in range(ny // strip):
            here = slice(strip * r, strip * (r + 1))
            s = [stress[c, x + 1, here] for c in range(6)]
            before = [stress[c, x, here] for c in (0, 3, 4)]
            if with_source:
                extra = source[x + 1, here]
                s[:3] = [value + extra for value in s[:3]]
                before[0] = before[0] + source[x, here]
            s_xx, s_yy, s_zz, s_xy, s_xz, s_yz = s
            rolled = [pltpu.roll(value, 1, 0) for value in (s_xy, s_yy, s_yz)]
            up = [jnp.where(top, above[c], rolled[c]) for c in range(3)]
            factor = time_step * cells[0, x, here]
            sums = (
                (s_xx - before[0]) + (s_xy - up[0]) + (s_xz - shifted_up(s_xz)),
                (s_xy - before[1]) + (s_yy - up[1]) + (s_yz - shifted_up(s_yz)),
                (s_xz - before[2]) + (s_yz - up[2]) + (s_zz - shifted_up(s_zz)),
            )
            for c in range(3):
                velocity[c, x, here] = velocity[c, x, here] + factor * sums[c]
            above = rolled

    def stress_plane(x, strips=range(ny // strip)):
        if strips[-1] == ny // strip - 1:
            below = [upper_rows[c, pl.ds(x, 1)] for c in range(3)]
        else:
            following = strip * (strips[-1] + 1)
            below = [velocity[c, x, following : following + 1] for c in range(3)]
        below = [jnp.broadcast_to(row, (strip, nz)) for row in below]
        for r in reversed(strips):
            here = slice(strip * r, strip * (r + 1))
            v = [velocity[c, x, here] for c in range(3)]
            rolled = [pltpu.roll(value, strip - 1, 0) for value in v]
            in_x = [velocity[c, x + 1, here] - v[c] for c in range(3)]
            in_y = [jnp.where(bottom, below[c], rolled[c]) - v[c] for c in range(3)]
            in_z = [shifted_down(v[c]) - v[c] for c in range(3)]
            decay = jnp.exp(-time_step * cells[3, x, here])
            shear = time_step * cells[2, x, here]
            normal = [in_x[0], in_y[1], in_z[2]]
            common = time_step * cells[1, x, here] * (normal[0] + normal[1] + normal[2])
            twice = 2.0 * shear
            if with_source:
                extra = source[x + 1, here]
                common = common + extra
            values = []
            for c in range(3):
                value = decay * (stress[c, x + 1, here] + (common + twice * normal[c]))
                values.append(value + extra if with_source else value)
            for c, (a, b) in enumerate(
                ((in_y[0], in_x[1]), (in_z[0], in_x[2]), (in_z[1], in_y[2])), 3
            ):
                values.append(decay * (stress[c, x + 1, here] + shear * (a + b)))
            for c in range(6):
                stress[c, x + 1, here] = values[c]
            if not with_source and r == ny // strip - 1:
                for c, which in enumerate((3, 1, 5)):
                    last_rows[c, pl.ds(x, 1)] = values[which][strip - 1 :]
            below = rolled

    def one_chunk(n, _):
        k = chunks - 1 - n

        if not with_source:

            @pl.when(k > 0)
            def _():
                for copy in arriving(k - 1):
                    copy.wait()

        def one_plane(m, _):
            x = k * per + (per - 1 - m)
            if kind in ("first", "velocity"):
                velocity_plane(x)
            if kind == "first":
                stress_plane(x)
            elif kind == "inner":
                stress_plane(x, range(ny // strip - 1))
            elif kind == "outer":
                stress_plane(x, range(ny // strip - 1, ny // strip))
            return 0

        lax.fori_loop(0, per, one_plane, 0, unroll=True)
        if kind in ("inner", "outer"):
            for copy in leaving(k):
                copy.start()
        return 0

    if kind == "first":
        for copy in arriving(chunks - 1):
            copy.wait()
    more = []
    if kind == "inner":
        more.append(
            pltpu.make_async_copy(velocity.at[:, 0:nx], out_velocity, out_sems.at[chunks])
        )
        more[0].start()
        for m in range(per - 1):
            stress_plane(nx - 2 - m, range(ny // strip - 1))
        more += leaving(chunks - 1, 0, per - 1)
        more[1].start()
        lax.fori_loop(1, chunks, one_chunk, 0)
    elif kind == "outer":
        stress_plane(nx - 1, range(ny // strip - 1))
        move = (stress.at[:, nx, 0:inner], out_stress.at[:, nx - 1, 0:inner])
        more.append(pltpu.make_async_copy(*move, out_sems.at[chunks]))
        more[0].start()
        lax.fori_loop(0, chunks, one_chunk, 0)
    else:
        lax.fori_loop(0, chunks, one_chunk, 0)
    if kind in ("inner", "outer"):

        def done(n, _):
            for copy in leaving(n):
                copy.wait()
            return 0

        lax.fori_loop(0, chunks - (kind == "inner"), done, 0)
        for copy in more:
            copy.wait()
    if kind == "first":
        for c, which in enumerate((0, 3, 4)):
            last_plane[c] = stress[which, nx]
        last_plane[3] = cells[3, nx - 1]
        last_rows[3] = cells[3, :nx, ny - 1]
        partial_velocity(
            [stress[c, 1] for c in range(6)],
            [velocity[c, 0] for c in range(3)],
            time_step * cells[0, 0],
            part_plane,
            (nothing, row_before),
        )
        partial_velocity(
            [stress[c, 1:, 0] for c in range(6)],
            [velocity[c, :nx, 0] for c in range(3)],
            time_step * cells[0, :nx, 0],
            part_rows,
            (row_before, nothing),
        )


def estimate(nx, ny, nz, words):
    count = nx * ny * nz
    return pl.CostEstimate(
        flops=100 * count, bytes_accessed=4 * words * count, transcendentals=count
    )


def first_step(stress, velocity, coefficients, plane, rows, upper_plane, upper_rows):
    _, nx, ny, nz = velocity.shape
    fields = [in_hbm(a) for a in (stress, velocity, *coefficients)]
    on_chip = pl.BlockSpec(memory_space=pltpu.VMEM)
    return pl.pallas_call(
        functools.partial(step_kernel, "first"),
        in_specs=[pl.BlockSpec(memory_space=pltpu.HBM)] * len(fields) + [on_chip] * 4,
        out_specs=(on_chip,) * 7,
        out_shape=(
            *[pltpu.VMEM((n, nx + 1, ny, nz), jnp.float32) for n in (6, 3, 4)],
            *[f32(n, m, nz) for n in (4, 3) for m in (ny, nx)],
        ),
        scratch_shapes=[pltpu.SemaphoreType.DMA((nx // per, len(fields)))],
        compiler_params=pltpu.CompilerParams(vmem_limit_bytes=20 << 20),
        cost_estimate=estimate(nx, ny, nz, 13),
        name="first_step",
    )(*fields, plane, rows, upper_plane, upper_rows)


def second_step(kind, stress, velocity, cells, source, edges=(), outside=None):
    nx, ny, nz = cells.shape[1] - 1, *cells.shape[2:]
    held = [in_vmem(a) for a in (stress, velocity, cells, source)]
    on_chip, off_chip = [pl.BlockSpec(memory_space=m) for m in (pltpu.VMEM, pltpu.HBM)]
    in_specs = [on_chip] * (len(held) + len(edges))
    state = [pltpu.VMEM(a.shape, jnp.float32) for a in (stress, velocity)]
    out = [pltpu.HBM((n, nx, ny, nz), jnp.float32) for n in (6, 3)]
    args, sems = (*held, *edges), [pltpu.SemaphoreType.DMA((nx // per + 1,))]
    if kind == "velocity":
        out_shape, out_specs, aliases, sems = (state[1],), (on_chip,), {1: 0}, []
    elif kind == "inner":
        out_shape = (out[0], *state, out[1])
        out_specs, aliases = (off_chip, on_chip, on_chip, off_chip), {0: 1, 1: 2}
    else:
        out_shape, out_specs = (out[0], *state), (off_chip, on_chip, on_chip)
        aliases = {0: 1, 1: 2, len(args): 0}
        in_specs, args = in_specs + [off_chip], (*args, in_hbm(outside))
    return pl.pallas_call(
        functools.partial(step_kernel, kind),
        in_specs=in_specs,
        out_specs=out_specs,
        out_shape=out_shape,
        input_output_aliases=aliases,
        scratch_shapes=sems,
        compiler_params=pltpu.CompilerParams(vmem_limit_bytes=20 << 20),
        cost_estimate=estimate(nx, ny, nz, 3),
        name="second_" + kind,
    )(*args)


def shards(
    source_planes,
    weight_x,
    weight_y,
    weight_z,
    box_anchor,
    velocity,
    stress,
    lame_lambda,
    lame_mu,
    buoyancy,
    attenuation,
):
    nx, ny, nz = lame_mu.shape
    box_x, sources = weight_x.shape
    box_y = weight_y.shape[0]
    size_x, size_y = lax.axis_size("gx"), lax.axis_size("gy")
    own = source_planes.shape[0]
    columns = box_y // ny
    part = ny // size_x
    coefficients = (buoyancy, lame_lambda, lame_mu, attenuation)

    fields = (stress, velocity, buoyancy)
    pieces, send_x, send_y, *parts = sections(
        source_planes, weight_y, weight_z, fields, size_x, size_y, columns
    )
    pieces = pieces.reshape(sources, part, lanes)
    gathered = lax.all_to_all(pieces, ("gx", "gy"), 0, 0, tiled=True)
    plane = neighbour(send_x, "gx", 1)
    rows = neighbour(send_y, "gy", 1)

    gathered = gathered.reshape(sources * part, lanes)
    shares, first_x, first_y = contract(
        box_anchor, weight_x, gathered, (*parts, plane, rows), own, part, nx, size_x
    )
    box = lax.all_to_all(shares, "gx", 0, 0, tiled=True)
    upper_x = neighbour(first_x, "gx", -1)
    upper_y = neighbour(first_y, "gy", -1)
    box, upper_x, upper_y = lax.optimization_barrier((box, upper_x, upper_y))

    strained, speed, cells, last_x, last_y, *parts[:2] = first_step(
        stress, velocity, coefficients, plane, rows, upper_x, upper_y
    )
    lower_x = neighbour(last_x, "gx", 1)
    lower_y = neighbour(last_y, "gy", 1)
    source = place(box_anchor, box, cells, part, weight_z.shape[0])
    (speed,) = second_step("velocity", strained, speed, cells, source[0])
    speed, lower_x, lower_y = lax.optimization_barrier((speed, lower_x, lower_y))
    first_x, first_y = second_edges(parts, lower_x, lower_y, source)
    upper_x = neighbour(first_x, "gx", -1)
    upper_y = neighbour(first_y, "gy", -1)
    partly, strained, speed, velocity_out = second_step(
        "inner", strained, speed, cells, source[0], (first_x, first_y)
    )
    stress_out, _, _ = second_step(
        "outer", strained, speed, cells, source[0], (upper_x, upper_y), partly
    )
    return (velocity_out, stress_out)


def solution(mesh):
    in_specs = (
        P(("gx", "gy"), None, None),
        P(),
        P(),
        P(),
        P(),
        P(None, "gx", "gy", None),
        P(None, "gx", "gy", None),
        P("gx", "gy", None),
        P("gx", "gy", None),
        P("gx", "gy", None),
        P("gx", "gy", None),
    )
    out_specs = (P(None, "gx", "gy", None), P(None, "gx", "gy", None))
    return jax.shard_map(shards, mesh=mesh, in_specs=in_specs, out_specs=out_specs, check_vma=False)
```

```python
import functools

import jax
import jax.numpy as jnp
from jax import lax
from jax.experimental import pallas as pl
from jax.experimental.pallas import tpu as pltpu
from jax.sharding import PartitionSpec as P

time_step = 0.2
strip = 8
lanes = 128
per = 2


def neighbour(value, axis, by):
    size = lax.axis_size(axis)
    pairs = [(i, i + by) for i in range(size) if 0 <= i + by < size]
    return lax.ppermute(value, axis, pairs)


def in_hbm(value):
    return pltpu.with_memory_space_constraint(value, pltpu.HBM)


def in_vmem(value):
    return pltpu.with_memory_space_constraint(value, pltpu.VMEM)


def f32(*shape):
    return jax.ShapeDtypeStruct(shape, jnp.float32)


def split(values, parts=2):
    out = []
    for _ in range(parts):
        out.append(values.astype(jnp.bfloat16))
        values = values - out[-1].astype(jnp.float32)
    return out


def dot(a, b, contract=((1,), (0,))):
    return sum(
        lax.dot_general(
            a[i], b[j], (contract, ((), ())), preferred_element_type=jnp.float32
        )
        for i, j in sorted(
            ((i, j) for i in range(len(a)) for j in range(len(b))), key=lambda ij: -sum(ij)
        )
        if i + j < max(len(a), len(b))
    )


def shifted_up(values):
    first = jnp.zeros((values.shape[0], 1), jnp.float32)
    return jnp.concatenate([first, values[:, :-1]], 1)


def shifted_down(values):
    last = jnp.zeros((values.shape[0], 1), jnp.float32)
    return jnp.concatenate([values[:, 1:], last], 1)


def after_row(values, row):
    where = lax.broadcasted_iota(jnp.int32, values.shape, 0)
    return jnp.where(where == 0, row, pltpu.roll(values, 1, 0))


def partial_velocity(stress, velocity, factor, out, before):
    xx, yy, zz, xy, xz, yz = stress
    along_x, along_y = before
    out[0] = velocity[0] + factor * (
        (xx - along_x(xx)) + (xy - along_y(xy)) + (xz - shifted_up(xz))
    )
    out[1] = velocity[1] + factor * (
        (xy - along_x(xy)) + (yy - along_y(yy)) + (yz - shifted_up(yz))
    )
    out[2] = velocity[2] + factor * (
        (xz - along_x(xz)) + (yz - along_y(yz)) + (zz - shifted_up(zz))
    )


def nothing(values):
    return jnp.zeros_like(values)


def row_before(values):
    return after_row(values, 0.0)


def edges_kernel(between, stress, velocity, buoyancy, *refs):
    out_plane, out_rows, part_plane, part_rows, b_plane, b_rows = refs[:6]
    s_plane, s_rows, v_plane, v_rows, sems = refs[6:]
    _, nx, ny, _ = stress.shape
    moves = [
        (stress.at[:, 0], s_plane),
        (stress.at[:, :, 0], s_rows),
        (velocity.at[:, 0], v_plane),
        (velocity.at[:, :, 0], v_rows),
        (buoyancy.at[0], b_plane),
        (buoyancy.at[:, 0], b_rows),
        (stress.at[0, nx - 1], out_plane.at[0]),
        (stress.at[3:5, nx - 1], out_plane.at[1:3]),
        (stress.at[3, :, ny - 1], out_rows.at[0]),
        (stress.at[1, :, ny - 1], out_rows.at[1]),
        (stress.at[5, :, ny - 1], out_rows.at[2]),
    ]
    copies = [pltpu.make_async_copy(*move, sems.at[k]) for k, move in enumerate(moves)]
    for copy in copies:
        copy.start()
    between()
    for copy in copies:
        copy.wait()
    partial_velocity(
        [s_plane[c] for c in range(6)],
        [v_plane[c] for c in range(3)],
        time_step * b_plane[...],
        part_plane,
        (nothing, row_before),
    )
    partial_velocity(
        [s_rows[c] for c in range(6)],
        [v_rows[c] for c in range(3)],
        time_step * b_rows[...],
        part_rows,
        (row_before, nothing),
    )


def take_halo(part_plane, part_rows, b_plane, b_rows, plane, rows, out_plane, out_rows):
    factor_plane, factor_rows = time_step * b_plane[...], time_step * b_rows[...]
    for c in range(3):
        first_row = lax.broadcasted_iota(jnp.int32, factor_plane.shape, 0) == 0
        corner = jnp.where(first_row, rows[c, 0:1], 0.0)
        out_plane[c] = part_plane[c] - factor_plane * (plane[c] + corner)
        first_row = lax.broadcasted_iota(jnp.int32, factor_rows.shape, 0) == 0
        corner = jnp.where(first_row, plane[c, 0:1], 0.0)
        out_rows[c] = part_rows[c] - factor_rows * (rows[c] + corner)


def sections_kernel(size_x, size_y, columns, *refs):
    planes, weight_y, weight_z = refs[:3]
    out, (held, planes_in, y_in, z_in, sems) = refs[6], refs[13:18]
    own = planes.shape[0]
    box_y, box_z = weight_y.shape[0], weight_z.shape[0]
    part = box_y // (columns * size_x)
    moves = [(weight_y, y_in), (weight_z, z_in)]
    moves += [(planes.at[t], planes_in.at[t]) for t in range(own)]
    copies = [pltpu.make_async_copy(*move, sems.at[k]) for k, move in enumerate(moves)]
    for copy in copies:
        copy.start()

    def products():
        out[...] = jnp.zeros_like(out)
        held[...] = jnp.zeros_like(held)
        copies[0].wait()
        copies[1].wait()
        in_y, in_z = split(y_in[...]), split(z_in[...])
        for t in range(own):
            copies[2 + t].wait()
            partly = split(dot(in_y, split(planes_in[t])))
            held[t, strip : strip + box_y, :box_z] = dot(partly, in_z, ((1,), (1,)))
        free = lax.broadcasted_iota(jnp.int32, (1, lanes), 1) >= box_z
        width = lanes - box_z
        for k in range(columns):
            for i in range(size_x):
                start = strip + (k * size_x + i) * part
                device = i * size_y + size_y - columns + k
                for t in range(own):
                    row = (device * own + t) * part
                    out[row : row + part] = held[t, start : start + part]
                    for p in range(box_z // width if i == 0 and k > 0 else 0):
                        ahead = pltpu.roll(held[t, start - 1 : start], box_z - p * width, 1)
                        here = held[t, start + p : start + p + 1]
                        out[row + p : row + p + 1] = jnp.where(free, ahead, here)

    edges_kernel(products, *refs[3:6], *refs[7:13], *refs[18:])


def sections(planes, weight_y, weight_z, fields, size_x, size_y, columns):
    own, box_y = planes.shape[0], weight_y.shape[0]
    height = own * (box_y // (columns * size_x))
    nx, ny, nz = fields[2].shape
    on_chip = lambda *shape: pltpu.VMEM(shape, jnp.float32)
    return pl.pallas_call(
        functools.partial(sections_kernel, size_x, size_y, columns),
        in_specs=[pl.BlockSpec(memory_space=pltpu.HBM)] * 6,
        out_shape=(
            f32(size_x * size_y * height, lanes),
            f32(3, ny, nz),
            f32(3, nx, nz),
            f32(3, ny, nz),
            f32(3, nx, nz),
            f32(ny, nz),
            f32(nx, nz),
        ),
        scratch_shapes=[
            on_chip(own, strip + box_y, lanes),
            *[on_chip(*a.shape) for a in (planes, weight_y, weight_z)],
            pltpu.SemaphoreType.DMA((2 + own,)),
            on_chip(6, ny, nz),
            on_chip(6, nx, nz),
            on_chip(3, ny, nz),
            on_chip(3, nx, nz),
            pltpu.SemaphoreType.DMA((11,)),
        ],
        compiler_params=pltpu.CompilerParams(vmem_limit_bytes=16 << 20),
        name="sections",
    )(*map(in_hbm, (planes, weight_y, weight_z, *fields)))


def contract_kernel(own, part, nx, anchor, weight_x, gathered, *refs):
    out, padded = refs[6], refs[9]
    take_halo(*refs[:6], *refs[7:9])
    box_x, count = weight_x.shape
    size_x = out.shape[0]
    span = nx + 1
    devices = count // own
    stride = own * part
    section = lax.broadcasted_iota(jnp.int32, (count, count), 0)
    column = lax.broadcasted_iota(jnp.int32, (count, count), 1)
    pick = section == own * lax.rem(column, devices) + lax.div(column, devices)
    pick = pick.astype(jnp.bfloat16)
    weights = [dot([w], [pick]).astype(jnp.bfloat16) for w in split(weight_x[...])]
    padded[...] = jnp.zeros_like(padded)
    for r in range(part):
        terms = [gathered[pl.ds(t * part + r, devices, stride=stride), :] for t in range(own)]
        box = dot(weights, split(jnp.concatenate(terms, 0)))
        padded[r, pl.ds(anchor[0] + strip, box_x), :] = box
    for i in range(size_x):
        start = strip + i * nx
        for r in range(part):
            out[i, r * span : r * span + nx] = padded[r, start : start + nx]
            out[i, r * span + nx : (r + 1) * span] = padded[r, start - 1 : start]
        left = out.shape[1] - part * span
        out[i, part * span :] = jnp.zeros((left, lanes), jnp.float32)


def contract(anchor, weight_x, gathered, edges, own, part, nx, size_x):
    height = -(-part * (nx + 1) // strip) * strip
    return pl.pallas_call(
        functools.partial(contract_kernel, own, part, nx),
        in_specs=[pl.BlockSpec(memory_space=pltpu.SMEM)]
        + [pl.BlockSpec(memory_space=pltpu.VMEM)] * (2 + len(edges)),
        out_shape=(
            f32(size_x, height, lanes),
            f32(*edges[0].shape),
            f32(*edges[1].shape),
        ),
        scratch_shapes=[pltpu.VMEM((part, 2 * strip + size_x * nx, lanes), jnp.float32)],
        compiler_params=pltpu.CompilerParams(vmem_limit_bytes=16 << 20),
        name="contract",
    )(anchor, weight_x, gathered, *edges)


def place_kernel(part, box_z, anchor, box, cells, *refs):
    out, out_plane, out_rows, held = refs
    size_x = box.shape[0]
    _, ny, nz = out.shape
    nx = out.shape[0] - 1
    span = nx + 1
    for i in range(size_x):
        for r in range(part):
            y = i * part + r
            first = r * span
            held[pl.ds(y, nx, stride=ny), :] = box[i, first : first + nx]
            held[nx * ny + y : nx * ny + y + 1] = box[i, first + nx : first + nx + 1]
    cell = lax.broadcasted_iota(jnp.int32, (lanes, nz), 1)
    which = lax.broadcasted_iota(jnp.int32, (lanes, nz), 0)
    pick = ((cell - anchor[2] == which) & (which < box_z)).astype(jnp.bfloat16)

    def placed(values):
        return (-time_step) * dot(split(values, 3), [pick])

    for t in range(0, nx, 4):
        values = placed(held[t * ny : (t + 4) * ny])
        for u in range(4):
            decay = jnp.exp(-time_step * cells[3, t + u])
            out[t + u + 1] = decay * values[u * ny : (u + 1) * ny]
    out[0] = jnp.zeros((ny, nz), jnp.float32)
    out_plane[...] = placed(held[nx * ny :])
    width = lanes - box_z
    piece = lax.div(lax.broadcasted_iota(jnp.int32, (nx, lanes), 1), width)
    ahead = jnp.zeros((nx, lanes), jnp.float32)
    for p in range(box_z // width):
        values = pltpu.roll(box[0, p * span : p * span + nx], lanes - box_z + p * width, 1)
        ahead = jnp.where(piece == p, values, ahead)
    out_rows[...] = placed(ahead)


def place(anchor, box, cells, part, box_z):
    nx, ny, nz = cells.shape[1] - 1, *cells.shape[2:]
    on_chip = pl.BlockSpec(memory_space=pltpu.VMEM)
    return pl.pallas_call(
        functools.partial(place_kernel, part, box_z),
        in_specs=[pl.BlockSpec(memory_space=pltpu.SMEM)] + [on_chip] * 2,
        out_specs=(on_chip,) * 3,
        out_shape=(pltpu.VMEM((nx + 1, ny, nz), jnp.float32), f32(ny, nz), f32(nx, nz)),
        scratch_shapes=[pltpu.VMEM(((nx + 1) * ny, lanes), jnp.float32)],
        compiler_params=pltpu.CompilerParams(vmem_limit_bytes=12 << 20),
        name="place",
    )(anchor, box, in_vmem(cells))


def second_edges_kernel(*refs):
    part_plane, part_rows, b_plane, b_rows, plane, rows = refs[:6]
    source, box_plane, box_rows, first_plane, first_rows = refs[6:]
    take_halo(part_plane, part_rows, b_plane, b_rows, plane, rows, first_plane, first_rows)
    q_plane = jnp.exp(-time_step * plane[3]) * box_plane[...]
    q_rows = jnp.exp(-time_step * rows[3]) * box_rows[...]
    factor = time_step * b_plane[...]
    own = source[1]
    first_plane[0] = first_plane[0] + factor * (own - q_plane)
    first_plane[1] = first_plane[1] + factor * (own - after_row(own, q_rows[0:1]))
    first_plane[2] = first_plane[2] + factor * (own - shifted_up(own))
    factor = time_step * b_rows[...]
    own = source[1:, 0]
    first_rows[0] = first_rows[0] + factor * (own - after_row(own, q_plane[0:1]))
    first_rows[1] = first_rows[1] + factor * (own - q_rows)
    first_rows[2] = first_rows[2] + factor * (own - shifted_up(own))


def second_edges(parts, plane, rows, source):
    on_chip = pl.BlockSpec(memory_space=pltpu.VMEM)
    return pl.pallas_call(
        second_edges_kernel,
        in_specs=[on_chip] * 9,
        out_specs=(on_chip,) * 2,
        out_shape=tuple(f32(*a.shape) for a in parts[:2]),
        compiler_params=pltpu.CompilerParams(vmem_limit_bytes=8 << 20),
        name="second_edges",
    )(*parts, plane, rows, in_vmem(source[0]), *source[1:])


def step_kernel(kind, *refs):
    with_source = kind != "first"
    if kind == "velocity":
        stress, cells, source, velocity = refs[0], refs[2], refs[3], refs[4]
    elif kind == "inner":
        cells, source, first_plane, first_rows = refs[2:6]
        out_stress, stress, velocity, out_velocity, out_sems = refs[6:]
    elif kind == "outer":
        cells, source, upper_plane, upper_rows = refs[2:6]
        out_stress, stress, velocity, out_sems = refs[7:]
    else:
        fields, (plane, rows, upper_plane, upper_rows) = refs[:6], refs[6:10]
        stress, velocity, cells, last_plane, last_rows, part_plane, part_rows = refs[10:17]
        in_sems = refs[17]
    nx, ny, nz = cells.shape[1] - 1, *cells.shape[2:]
    chunks = nx // per

    def arriving(k):
        here, above = pl.ds(k * per, per), pl.ds(k * per + 1, per)
        moves = [
            (fields[0].at[:, here], stress.at[:, above]),
            (fields[1].at[:, here], velocity.at[:, here]),
        ]
        for n, field in enumerate(fields[2:6]):
            moves.append((field.at[here], cells.at[n, here]))
        return [pltpu.make_async_copy(*m, in_sems.at[k, n]) for n, m in enumerate(moves)]

    inner = ny - strip

    def leaving(k, first=0, count=per):
        across = slice(0, inner) if kind == "inner" else slice(inner, ny)
        here = pl.ds(k * per + first, count)
        above = pl.ds(k * per + first + 1, count)
        move = (stress.at[:, above, across], out_stress.at[:, here, across])
        return [pltpu.make_async_copy(*move, out_sems.at[k])]

    def every(make, act):
        def one(n, _):
            for copy in make(chunks - 1 - n):
                act(copy)
            return 0

        lax.fori_loop(0, chunks, one, 0)

    if not with_source:
        every(arriving, lambda copy: copy.start())
    if kind == "first":
        for c, which in enumerate((0, 3, 4)):
            stress[which, 0] = plane[c]
    if kind in ("first", "outer"):
        for c in range(3):
            velocity[c, nx] = upper_plane[c]
    if kind == "inner":
        for c in range(3):
            velocity[c, 0] = first_plane[c]
            velocity[c, :nx, 0] = first_rows[c]

    top = lax.broadcasted_iota(jnp.int32, (strip, nz), 0) == 0
    bottom = lax.broadcasted_iota(jnp.int32, (strip, nz), 0) == strip - 1

    def velocity_plane(x):
        above = [jnp.zeros((strip, nz), jnp.float32)] * 3
        if not with_source:
            above = [jnp.broadcast_to(rows[c, pl.ds(x, 1)], (strip, nz)) for c in range(3)]
        for r in range(ny // strip):
            here = slice(strip * r, strip * (r + 1))
            s = [stress[c, x + 1, here] for c in range(6)]
            before = [stress[c, x, here] for c in (0, 3, 4)]
            if with_source:
                extra = source[x + 1, here]
                s[:3] = [value + extra for value in s[:3]]
                before[0] = before[0] + source[x, here]
            s_xx, s_yy, s_zz, s_xy, s_xz, s_yz = s
            rolled = [pltpu.roll(value, 1, 0) for value in (s_xy, s_yy, s_yz)]
            up = [jnp.where(top, above[c], rolled[c]) for c in range(3)]
            factor = time_step * cells[0, x, here]
            sums = (
                (s_xx - before[0]) + (s_xy - up[0]) + (s_xz - shifted_up(s_xz)),
                (s_xy - before[1]) + (s_yy - up[1]) + (s_yz - shifted_up(s_yz)),
                (s_xz - before[2]) + (s_yz - up[2]) + (s_zz - shifted_up(s_zz)),
            )
            for c in range(3):
                velocity[c, x, here] = velocity[c, x, here] + factor * sums[c]
            above = rolled

    def stress_plane(x, strips=range(ny // strip)):
        if strips[-1] == ny // strip - 1:
            below = [upper_rows[c, pl.ds(x, 1)] for c in range(3)]
        else:
            following = strip * (strips[-1] + 1)
            below = [velocity[c, x, following : following + 1] for c in range(3)]
        below = [jnp.broadcast_to(row, (strip, nz)) for row in below]
        for r in reversed(strips):
            here = slice(strip * r, strip * (r + 1))
            v = [velocity[c, x, here] for c in range(3)]
            rolled = [pltpu.roll(value, strip - 1, 0) for value in v]
            in_x = [velocity[c, x + 1, here] - v[c] for c in range(3)]
            in_y = [jnp.where(bottom, below[c], rolled[c]) - v[c] for c in range(3)]
            in_z = [shifted_down(v[c]) - v[c] for c in range(3)]
            decay = jnp.exp(-time_step * cells[3, x, here])
            shear = time_step * cells[2, x, here]
            normal = [in_x[0], in_y[1], in_z[2]]
            common = time_step * cells[1, x, here] * (normal[0] + normal[1] + normal[2])
            twice = 2.0 * shear
            if with_source:
                extra = source[x + 1, here]
                common = common + extra
            values = []
            for c in range(3):
                value = decay * (stress[c, x + 1, here] + (common + twice * normal[c]))
                values.append(value + extra if with_source else value)
            for c, (a, b) in enumerate(
                ((in_y[0], in_x[1]), (in_z[0], in_x[2]), (in_z[1], in_y[2])), 3
            ):
                values.append(decay * (stress[c, x + 1, here] + shear * (a + b)))
            for c in range(6):
                stress[c, x + 1, here] = values[c]
            below = rolled

    def one_chunk(n, _):
        k = chunks - 1 - n

        if not with_source:

            @pl.when(k > 0)
            def _():
                for copy in arriving(k - 1):
                    copy.wait()

        def one_plane(m, _):
            x = k * per + (per - 1 - m)
            if kind in ("first", "velocity"):
                velocity_plane(x)
            if kind == "first":
                stress_plane(x)
            elif kind == "inner":
                stress_plane(x, range(ny // strip - 1))
            elif kind == "outer":
                stress_plane(x, range(ny // strip - 1, ny // strip))
            return 0

        lax.fori_loop(0, per, one_plane, 0, unroll=True)
        if kind in ("inner", "outer"):
            for copy in leaving(k):
                copy.start()
        return 0

    if kind == "first":
        for copy in arriving(chunks - 1):
            copy.wait()
    more = []
    if kind == "inner":
        more.append(
            pltpu.make_async_copy(velocity.at[:, 0:nx], out_velocity, out_sems.at[chunks])
        )
        more[0].start()
        for m in range(per - 1):
            stress_plane(nx - 2 - m, range(ny // strip - 1))
        more += leaving(chunks - 1, 0, per - 1)
        more[1].start()
        lax.fori_loop(1, chunks, one_chunk, 0)
    elif kind == "outer":
        stress_plane(nx - 1, range(ny // strip - 1))
        move = (stress.at[:, nx, 0:inner], out_stress.at[:, nx - 1, 0:inner])
        more.append(pltpu.make_async_copy(*move, out_sems.at[chunks]))
        more[0].start()
        lax.fori_loop(0, chunks, one_chunk, 0)
    else:
        lax.fori_loop(0, chunks, one_chunk, 0)
    if kind in ("inner", "outer"):

        def done(n, _):
            for copy in leaving(n):
                copy.wait()
            return 0

        lax.fori_loop(0, chunks - (kind == "inner"), done, 0)
        for copy in more:
            copy.wait()
    if kind == "first":
        for c, which in enumerate((0, 3, 4)):
            last_plane[c] = stress[which, nx]
        last_plane[3] = cells[3, nx - 1]
        for c, which in enumerate((3, 1, 5)):
            last_rows[c] = stress[which, 1:, ny - 1]
        last_rows[3] = cells[3, :nx, ny - 1]
        partial_velocity(
            [stress[c, 1] for c in range(6)],
            [velocity[c, 0] for c in range(3)],
            time_step * cells[0, 0],
            part_plane,
            (nothing, row_before),
        )
        partial_velocity(
            [stress[c, 1:, 0] for c in range(6)],
            [velocity[c, :nx, 0] for c in range(3)],
            time_step * cells[0, :nx, 0],
            part_rows,
            (row_before, nothing),
        )


def estimate(nx, ny, nz, words):
    count = nx * ny * nz
    return pl.CostEstimate(
        flops=100 * count, bytes_accessed=4 * words * count, transcendentals=count
    )


def first_step(stress, velocity, coefficients, plane, rows, upper_plane, upper_rows):
    _, nx, ny, nz = velocity.shape
    fields = [in_hbm(a) for a in (stress, velocity, *coefficients)]
    on_chip = pl.BlockSpec(memory_space=pltpu.VMEM)
    return pl.pallas_call(
        functools.partial(step_kernel, "first"),
        in_specs=[pl.BlockSpec(memory_space=pltpu.HBM)] * len(fields) + [on_chip] * 4,
        out_specs=(on_chip,) * 7,
        out_shape=(
            *[pltpu.VMEM((n, nx + 1, ny, nz), jnp.float32) for n in (6, 3, 4)],
            *[f32(n, m, nz) for n in (4, 3) for m in (ny, nx)],
        ),
        scratch_shapes=[pltpu.SemaphoreType.DMA((nx // per, len(fields)))],
        compiler_params=pltpu.CompilerParams(vmem_limit_bytes=20 << 20),
        cost_estimate=estimate(nx, ny, nz, 13),
        name="first_step",
    )(*fields, plane, rows, upper_plane, upper_rows)


def second_step(kind, stress, velocity, cells, source, edges=(), outside=None):
    nx, ny, nz = cells.shape[1] - 1, *cells.shape[2:]
    held = [in_vmem(a) for a in (stress, velocity, cells, source)]
    on_chip, off_chip = [pl.BlockSpec(memory_space=m) for m in (pltpu.VMEM, pltpu.HBM)]
    in_specs = [on_chip] * (len(held) + len(edges))
    state = [pltpu.VMEM(a.shape, jnp.float32) for a in (stress, velocity)]
    out = [pltpu.HBM((n, nx, ny, nz), jnp.float32) for n in (6, 3)]
    args, sems = (*held, *edges), [pltpu.SemaphoreType.DMA((nx // per + 1,))]
    if kind == "velocity":
        out_shape, out_specs, aliases, sems = (state[1],), (on_chip,), {1: 0}, []
    elif kind == "inner":
        out_shape = (out[0], *state, out[1])
        out_specs, aliases = (off_chip, on_chip, on_chip, off_chip), {0: 1, 1: 2}
    else:
        out_shape, out_specs = (out[0], *state), (off_chip, on_chip, on_chip)
        aliases = {0: 1, 1: 2, len(args): 0}
        in_specs, args = in_specs + [off_chip], (*args, in_hbm(outside))
    return pl.pallas_call(
        functools.partial(step_kernel, kind),
        in_specs=in_specs,
        out_specs=out_specs,
        out_shape=out_shape,
        input_output_aliases=aliases,
        scratch_shapes=sems,
        compiler_params=pltpu.CompilerParams(vmem_limit_bytes=20 << 20),
        cost_estimate=estimate(nx, ny, nz, 3),
        name="second_" + kind,
    )(*args)


def shards(
    source_planes,
    weight_x,
    weight_y,
    weight_z,
    box_anchor,
    velocity,
    stress,
    lame_lambda,
    lame_mu,
    buoyancy,
    attenuation,
):
    nx, ny, nz = lame_mu.shape
    box_x, sources = weight_x.shape
    box_y = weight_y.shape[0]
    size_x, size_y = lax.axis_size("gx"), lax.axis_size("gy")
    own = source_planes.shape[0]
    columns = box_y // ny
    part = ny // size_x
    coefficients = (buoyancy, lame_lambda, lame_mu, attenuation)

    fields = (stress, velocity, buoyancy)
    pieces, send_x, send_y, *parts = sections(
        source_planes, weight_y, weight_z, fields, size_x, size_y, columns
    )
    pieces = pieces.reshape(sources, part, lanes)
    gathered = lax.all_to_all(pieces, ("gx", "gy"), 0, 0, tiled=True)
    plane = neighbour(send_x, "gx", 1)
    rows = neighbour(send_y, "gy", 1)

    gathered = gathered.reshape(sources * part, lanes)
    shares, first_x, first_y = contract(
        box_anchor, weight_x, gathered, (*parts, plane, rows), own, part, nx, size_x
    )
    box = lax.all_to_all(shares, "gx", 0, 0, tiled=True)
    upper_x = neighbour(first_x, "gx", -1)
    upper_y = neighbour(first_y, "gy", -1)
    box, upper_x, upper_y = lax.optimization_barrier((box, upper_x, upper_y))

    strained, speed, cells, last_x, last_y, *parts[:2] = first_step(
        stress, velocity, coefficients, plane, rows, upper_x, upper_y
    )
    lower_x = neighbour(last_x, "gx", 1)
    lower_y = neighbour(last_y, "gy", 1)
    source = place(box_anchor, box, cells, part, weight_z.shape[0])
    (speed,) = second_step("velocity", strained, speed, cells, source[0])
    speed, lower_x, lower_y = lax.optimization_barrier((speed, lower_x, lower_y))
    first_x, first_y = second_edges(parts, lower_x, lower_y, source)
    upper_x = neighbour(first_x, "gx", -1)
    upper_y = neighbour(first_y, "gy", -1)
    partly, strained, speed, velocity_out = second_step(
        "inner", strained, speed, cells, source[0], (first_x, first_y)
    )
    stress_out, _, _ = second_step(
        "outer", strained, speed, cells, source[0], (upper_x, upper_y), partly
    )
    return (velocity_out, stress_out)


def solution(mesh):
    in_specs = (
        P(("gx", "gy"), None, None),
        P(),
        P(),
        P(),
        P(),
        P(None, "gx", "gy", None),
        P(None, "gx", "gy", None),
        P("gx", "gy", None),
        P("gx", "gy", None),
        P("gx", "gy", None),
        P("gx", "gy", None),
    )
    out_specs = (P(None, "gx", "gy", None), P(None, "gx", "gy", None))
    return jax.shard_map(shards, mesh=mesh, in_specs=in_specs, out_specs=out_specs, check_vma=False)
```
